512 devices in a mesh: tm: 128 (over y, z, core), sy: 2 (over x_lo), sx: 2 (over x_hi).
Axes of the slice: x: 4 (x_hi: 2, x_lo: 2; x = x_hi * 2 + x_lo), y: 8, z: 8, core: 2. Of those that a mesh axis runs over, the one named last changes fastest.
Arguments:
- frames: bfloat16 [512, 32, 32, 256], P('tm', 'sy', 'sx'), may hold values from -6 to 6
- in_kernel: bfloat16 [5, 5, 256, 128], replicated, may hold values from -0.078125 to 0.078125
- dt_weight: bfloat16 [256], replicated, may hold values from -1 to 1
- rates: float32 [128], replicated
- out_kernel: bfloat16 [3, 3, 128, 256], replicated, may hold values from -0.1875 to 0.1875
- skip: float32 [256], replicated, may hold values from 0.1 to 1.9
Outputs:
- output: bfloat16 [512, 32, 32, 256], P('tm', 'sy', 'sx')
The draws below stay inside these ranges and needn't reach their ends.
All inputs are finite; a program needn't handle non-finite values.
Results may differ from the reference program's by a relative error of at most 0.001.
Values may be sent and summed in bfloat16 or wider, within the bound.
A program may use at most 128 MiB of HBM per device.

```python
import math
import jax
import jax.numpy as jnp
from jax import lax

C = 256
P_SIZE = 128
FRAMES = 512
HEIGHT = 32
WIDTH = 32


def draw_rates(key, part):
    logs = jax.random.uniform(key, (P_SIZE,), jnp.float32, math.log(0.0002), math.log(0.08))
    return jnp.exp(logs)


def shared_signs(key):
    flips = jax.random.randint(jax.random.fold_in(key, 101), (C,), 0, 2)
    return (2 * flips - 1).astype(jnp.float32)


def draw_dt_weight(key, part):
    signs = shared_signs(key)
    sizes = jax.random.uniform(jax.random.fold_in(key, 202), (C,), jnp.float32, 0.25, 0.75)
    return (signs * sizes / math.sqrt(C)).astype(jnp.bfloat16)


def draw_frames(key, part):
    signs = shared_signs(key)
    field_key = jax.random.fold_in(key, 303)
    noise_key = jax.random.fold_in(key, 404)
    shape = (FRAMES, HEIGHT, WIDTH, C)
    level = jax.random.uniform(field_key, (HEIGHT, WIDTH, 1), jnp.float32, -4.0, 3.0)
    noise = jax.random.truncated_normal(noise_key, -5.0, 5.0, shape, jnp.float32)
    mixed = noise + level * signs * (2.0 / math.sqrt(C))
    return jnp.clip(mixed, -6.0, 6.0).astype(jnp.bfloat16)


def normal_values(key, extent, spread, most, held_as=jnp.bfloat16):
    return jnp.clip(spread * jax.random.normal(key, extent, jnp.float32), -most, most).astype(held_as)


def setup_inputs(seed: int = 0) -> dict:
    key_of = jax.random.split(jax.random.key(seed), 7)
    return {
        "frames": draw_frames(jax.random.fold_in(key_of[6], 71), 0),
        "in_kernel": normal_values(key_of[1], (5, 5, C, P_SIZE), (25 * C) ** -0.5, 0.078125),
        "dt_weight": draw_dt_weight(jax.random.fold_in(key_of[6], 71), 0),
        "rates": draw_rates(jax.random.fold_in(key_of[6], 71), 0),
        "out_kernel": normal_values(key_of[4], (3, 3, P_SIZE, C), (9 * P_SIZE) ** -0.5, 0.1875),
        "skip": jnp.clip(1.0 + 0.18 * jax.random.normal(key_of[5], (C,), jnp.float32), 0.1, 1.9),
    }


def convolve(images, kernel, width):
    padded = jnp.pad(images.astype(jnp.float32), ((0, 0), (width, width), (width, width), (0, 0)))
    return lax.conv_general_dilated(padded, kernel.astype(jnp.float32), (1, 1), 'VALID', dimension_numbers=('NHWC', 'HWIO', 'NHWC'), precision=lax.Precision.HIGHEST)

def reference(frames, in_kernel, dt_weight, rates, out_kernel, skip):
    drive = convolve(frames, in_kernel, 2)
    step = jax.nn.softplus(jnp.dot(frames, dt_weight, preferred_element_type=jnp.float32))

    def advance(state, inputs):
        step_now, drive_now = inputs
        scaled = step_now[..., None] * rates
        state = jnp.exp(-scaled) * state + jnp.sqrt(-jnp.expm1(-2.0 * scaled)) * drive_now
        return (state, state)
    start = jnp.zeros((HEIGHT, WIDTH, P_SIZE), jnp.float32)
    _, hidden = lax.scan(advance, start, (step, drive))
    mixed = convolve(hidden, out_kernel, 1) + skip * frames.astype(jnp.float32)
    return mixed.astype(jnp.bfloat16)
```

```python
import jax
import jax.numpy as jnp
from jax import lax
from jax.experimental import pallas as pl
from jax.experimental.pallas import tpu as pltpu
from jax.sharding import PartitionSpec as P

ROW = 16
MESH = pl.DeviceIdType.MESH


def with_halo(block, sides, width):
    for axis, dim in sides:
        count = lax.axis_size(axis)
        forward = [(i, i + 1) for i in range(count - 1)]
        backward = [(target, source) for source, target in forward]
        low = lax.ppermute(
            lax.slice_in_dim(block, block.shape[dim] - width, None, axis=dim), axis, forward
        )
        high = lax.ppermute(lax.slice_in_dim(block, 0, width, axis=dim), axis, backward)
        block = jnp.concatenate([low, block, high], axis=dim)
    return block


def scan_kernel(cols, a_ref, b_ref, o_ref, ra, rb, ca, cb, ta, tb, outs, sems_a, sems_b, sems_ca, sems_cb, sems_o):
    me = lax.axis_index("tm")
    r = lax.rem(me, ROW)
    y = lax.div(me, ROW)
    base = me - r
    barrier = pltpu.get_barrier_semaphore()
    order = [8, 7, 9, 6, 10, 5, 11, 4, 12, 3, 13, 2, 14, 1, 15]
    peers = [lax.rem(r + d, ROW) for d in order]
    columns = [lax.rem(y + d, cols) for d in range(1, cols)]
    for p in peers:
        pl.semaphore_signal(barrier, inc=1, device_id={"tm": base + p}, device_id_type=MESH)
    for c in columns:
        pl.semaphore_signal(barrier, inc=1, device_id={"tm": c * ROW + r}, device_id_type=MESH)
    pl.semaphore_wait(barrier, ROW - 1 + cols - 1)

    def row_copy(src, dst, sems, p):
        return pltpu.make_async_remote_copy(
            src_ref=src, dst_ref=dst, send_sem=sems.at[0, p], recv_sem=sems.at[1, r],
            device_id={"tm": base + p}, device_id_type=MESH)

    def row_arrival(src, dst, sems, p):
        return pltpu.make_async_remote_copy(
            src_ref=src, dst_ref=dst, send_sem=sems.at[0, p], recv_sem=sems.at[1, p],
            device_id={"tm": base + p}, device_id_type=MESH)

    for p in peers:
        row_copy(a_ref.at[p], ra.at[r], sems_a, p).start()
        row_copy(b_ref.at[p], rb.at[r], sems_b, p).start()
    ra[r] = a_ref[r]
    rb[r] = b_ref[r]
    for p in peers:
        row_arrival(a_ref.at[p], ra.at[p], sems_a, p).wait()
        row_arrival(b_ref.at[p], rb.at[p], sems_b, p).wait()
    total_a = jnp.ones_like(ra[0])
    total_b = jnp.zeros_like(rb[0])
    before = []
    for k in range(ROW):
        before.append((total_a, total_b))
        here = ra[k]
        total_b = here * total_b + rb[k]
        total_a = total_a * here
    ta[...] = total_a
    tb[...] = total_b

    def column_copy(src, dst, sems, c, slot):
        return pltpu.make_async_remote_copy(
            src_ref=src, dst_ref=dst, send_sem=sems.at[0, c], recv_sem=sems.at[1, slot],
            device_id={"tm": c * ROW + r}, device_id_type=MESH)

    for c in columns:
        column_copy(ta, ca.at[y], sems_ca, c, y).start()
        column_copy(tb, cb.at[y], sems_cb, c, y).start()
    ca[y] = total_a
    cb[y] = total_b
    for c in columns:
        column_copy(ta, ca.at[c], sems_ca, c, c).wait()
        column_copy(tb, cb.at[c], sems_cb, c, c).wait()
    carry = jnp.zeros_like(total_b)
    for c in range(cols):
        carry = jnp.where(c < y, ca[c] * carry + cb[c], carry)
    for k in range(ROW):
        outs[k] = before[k][0] * carry + before[k][1]
    for p in peers:
        row_copy(outs.at[p], o_ref.at[r], sems_o, p).start()
    o_ref[r] = outs[r]
    for p in peers:
        row_arrival(outs.at[p], o_ref.at[p], sems_o, p).wait()


def prefix(decay, state):
    cols = lax.axis_size("tm") // ROW
    shape = (ROW, state.shape[0] * state.shape[1] // ROW, state.shape[2])
    chunk = shape[1:]
    vmem = pl.BlockSpec(memory_space=pltpu.VMEM)

    def kernel(*refs):
        scan_kernel(cols, *refs)

    result = pl.pallas_call(
        kernel,
        out_shape=jax.ShapeDtypeStruct(shape, jnp.float32),
        in_specs=[vmem, vmem],
        out_specs=vmem,
        scratch_shapes=[
            pltpu.VMEM((ROW,) + chunk, jnp.float32),
            pltpu.VMEM((ROW,) + chunk, jnp.float32),
            pltpu.VMEM((cols,) + chunk, jnp.float32),
            pltpu.VMEM((cols,) + chunk, jnp.float32),
            pltpu.VMEM(chunk, jnp.float32),
            pltpu.VMEM(chunk, jnp.float32),
            pltpu.VMEM((ROW,) + chunk, jnp.float32),
            pltpu.SemaphoreType.DMA((2, ROW)),
            pltpu.SemaphoreType.DMA((2, ROW)),
            pltpu.SemaphoreType.DMA((2, cols)),
            pltpu.SemaphoreType.DMA((2, cols)),
            pltpu.SemaphoreType.DMA((2, ROW)),
        ],
        compiler_params=pltpu.CompilerParams(collective_id=0, has_side_effects=True),
    )(decay.reshape(shape), state.reshape(shape))
    return result.reshape(state.shape)


def convolve(padded, kernel):
    return lax.conv_general_dilated(
        padded,
        kernel,
        (1, 1),
        "VALID",
        dimension_numbers=("NHWC", "HWIO", "NHWC"),
        preferred_element_type=jnp.float32,
    )


def convolve_exact(padded, kernel):
    return lax.conv_general_dilated(
        padded,
        kernel.astype(jnp.float32),
        (1, 1),
        "VALID",
        dimension_numbers=("NHWC", "HWIO", "NHWC"),
        precision=lax.Precision.HIGHEST,
        preferred_element_type=jnp.float32,
    )


def body(frames, in_kernel, dt_weight, rates, out_kernel, skip):
    widened = with_halo(frames, (("sy", 1), ("sx", 2)), 2)
    drive = convolve(widened, in_kernel)
    step = jax.nn.softplus(jnp.dot(frames, dt_weight, preferred_element_type=jnp.float32))
    count = frames.shape[0]
    state = jnp.zeros(drive.shape[1:], jnp.float32)
    summed = jnp.zeros(step.shape[1:], jnp.float32)
    locals_list = []
    summed_list = []
    for frame in range(count):
        scaled = step[frame][..., None] * rates
        state = jnp.exp(-scaled) * state + jnp.sqrt(-jnp.expm1(-2.0 * scaled)) * drive[frame]
        summed = summed + step[frame]
        locals_list.append(state)
        summed_list.append(summed)
    product = jnp.exp(-summed[..., None] * rates)
    incoming = prefix(product, state)
    hidden_list = []
    for frame in range(count):
        fixed = locals_list[frame] + jnp.exp(-summed_list[frame][..., None] * rates) * incoming
        hidden_list.append(fixed)
    hidden = jnp.stack(hidden_list, axis=0)
    rimmed = with_halo(hidden, (("sy", 1), ("sx", 2)), 1)
    mixed = convolve_exact(rimmed, out_kernel) + skip * frames.astype(jnp.float32)
    return mixed.astype(jnp.bfloat16)


def solution(mesh):
    return jax.shard_map(
        body,
        mesh=mesh,
        in_specs=(P("tm", "sy", "sx", None), P(), P(), P(), P(), P()),
        out_specs=P("tm", "sy", "sx", None),
        check_vma=False,
    )
```

```python
import jax
import jax.numpy as jnp
from jax import lax
from jax.experimental import pallas as pl
from jax.experimental.pallas import tpu as pltpu
from jax.sharding import PartitionSpec as P

ROW = 16
T, H, W = 4, 16, 16
PIX = H * W
C, S = 256, 128
MESH = pl.DeviceIdType.MESH
ORDER = [8, 7, 9, 6, 10, 5, 11, 4, 12, 3, 13, 2, 14, 1, 15]
F32 = jnp.float32
BF16 = jnp.bfloat16


def dot(a, b):
    return jnp.dot(a, b, preferred_element_type=F32)


def shifted(wide, taps, width, reach):
    rows = wide.shape[0]
    column = lax.rem(lax.broadcasted_iota(jnp.int32, (rows, width), 0), W)
    total = wide[:, reach * width:(reach + 1) * width]
    for tap in range(taps):
        move = tap - reach
        if move == 0:
            continue
        part = pltpu.roll(wide[:, tap * width:(tap + 1) * width], (-move) % rows, 0)
        inside = (column + move >= 0) & (column + move < W)
        total = total + jnp.where(inside, part, 0.0)
    return total


def one_minus_exp(u):
    series = u * (1.0 - u * (1 / 2) * (1.0 - u * (1 / 3) * (1.0 - u * (1 / 4) * (1.0 - u * (1 / 5) * (
        1.0 - u * (1 / 6) * (1.0 - u * (1 / 7) * (1.0 - u * (1 / 8))))))))
    return jnp.where(u < 0.5, series, 1.0 - jnp.exp(-u))


def layer_kernel(cols, frames, w1, dt, rates, w2, skip, out,
                 xp, wc, wc2, hr, hc, sc, gain, fade, drive, loc, hid, hr2, hc2, sc2, acc,
                 sa, sb, ra, rb, ca, cb, ta, tb, so, inc,
                 load, wload, w2load, halo, halo2, sems_a, sems_b, sems_ca, sems_cb, sems_o):
    me = lax.axis_index("tm")
    sy = lax.axis_index("sy")
    sx = lax.axis_index("sx")
    r = lax.rem(me, ROW)
    y = lax.div(me, ROW)
    base = me - r
    peers = [lax.rem(r + d, ROW) for d in ORDER]
    columns = [lax.rem(y + d, cols) for d in (4, 3, 5, 2, 6, 1, 7) if d < cols]
    near = [{"sy": 1 - sy}, {"sx": 1 - sx}, {"sy": 1 - sy, "sx": 1 - sx}]

    loads = [pltpu.make_async_copy(frames, xp.at[:, pl.ds(2, H)], load)]
    loads[0].start()
    wloads = []
    for i in range(25):
        wloads.append(pltpu.make_async_copy(
            w1.at[i], wc.at[pl.ds((i // 5) * C, C), pl.ds((i % 5) * S, S)], wload.at[i]))
    for c in wloads:
        c.start()
    w2loads = []
    for i in range(9):
        for half in range(2):
            w2loads.append(pltpu.make_async_copy(
                w2.at[i], wc2.at[pl.ds((i // 3) * C + half * S, S), pl.ds((i % 3) * C, C)],
                w2load.at[2 * i + half]))
    for c in w2loads:
        c.start()

    zrow = jnp.zeros((W, C), BF16)
    for f in range(T):
        for row in (0, 1, 18, 19):
            xp[f, row] = zrow
        hr[f, 2 * sy] = zrow
        hid[f, 0] = zrow
        hid[f, 17] = zrow
    for row in range(2):
        hc[18 * sy + row] = zrow
    hc2[17 * sy] = zrow

    barrier = pltpu.get_barrier_semaphore()
    targets = near + [{"tm": base + p} for p in peers] + [{"tm": c * ROW + r} for c in columns]
    for where in targets:
        pl.semaphore_signal(barrier, inc=1, device_id=where, device_id_type=MESH)

    loads[0].wait()
    row_id = lax.broadcasted_iota(jnp.int32, (PIX, 1), 0)
    slot = lax.rem(row_id, 16)
    edge = jnp.where(sx == 0, 15 - slot // 4, slot // 4)
    target = jnp.where(slot < 8, lax.rem(slot, 4) * PIX + (row_id // 16) * W + edge, -1)
    lane = lax.broadcasted_iota(jnp.int32, (PIX, PIX), 1)
    picked = jnp.zeros((PIX, C), F32)
    for f in range(T):
        pick = jnp.where(lane + f * PIX == target, 1.0, 0.0).astype(BF16)
        picked = picked + dot(pick, xp[f, pl.ds(2, H)].reshape(PIX, C))
    sc[...] = picked.astype(BF16).reshape(H, 16, C)

    def send(src, dst, sems, slot_out, slot_in, where):
        return pltpu.make_async_remote_copy(
            src_ref=src, dst_ref=dst, send_sem=sems.at[0, slot_out], recv_sem=sems.at[1, slot_in],
            device_id=where, device_id_type=MESH)

    pl.semaphore_wait(barrier, len(targets))
    halo_copies = [
        send(frames.at[:, pl.ds(14 * (1 - sy), 2)], hr.at[:, pl.ds(sy, 2)], halo, 0, 0, near[0]),
        send(sc, hc.at[pl.ds(2, H)], halo, 1, 1, near[1]),
        send(sc.at[pl.ds(14 * (1 - sy), 2)], hc.at[pl.ds(18 * sy, 2)], halo, 2, 2, near[2]),
    ]
    for c in halo_copies:
        c.start()

    weight = jnp.broadcast_to(dt[...].reshape(1, C), (S, C))
    speed = rates[...]
    faded = None
    for f in range(T):
        v = lax.dot_general(xp[f, pl.ds(2, H)].reshape(PIX, C), weight, (((1,), (1,)), ((), ())),
                            preferred_element_type=F32)
        scaled = (jnp.maximum(v, 0.0) + jnp.log1p(jnp.exp(-jnp.abs(v)))) * speed
        decay = jnp.exp(-scaled)
        gain[f] = jnp.sqrt(one_minus_exp(2.0 * scaled))
        loc[f] = decay
        faded = decay if f == 0 else faded * decay
        fade[f] = faded
    sa[...] = faded.reshape(ROW, H, S)
    for p in peers:
        send(sa.at[p], ra.at[r], sems_a, p, r, {"tm": base + p}).start()
    ra[r] = sa[r]

    for c in wloads:
        c.wait()
    for f in range(T):
        left = jnp.concatenate([xp[f, pl.ds(dy, H)].reshape(PIX, C) for dy in range(5)], axis=1)
        drive[f] = shifted(dot(left, wc[...]), 5, S, 2)

    for c in halo_copies:
        c.wait()
    left = jnp.concatenate([hr[:, pl.ds(k, 2)].reshape(T * 2 * W, C) for k in range(2)], axis=1)
    first = pl.multiple_of(3 * C * (1 - sy), C)
    extra = shifted(dot(left, wc[pl.ds(first, 2 * C), :]), 5, S, 2).reshape(T, 2 * W, S)
    at = pl.multiple_of(14 * W * (1 - sy), 2 * W)
    for f in range(T):
        drive[f, pl.ds(at, 2 * W), :] += extra[f]
    left = jnp.concatenate([hc[pl.ds(dy, H)].reshape(PIX, C) for dy in range(5)], axis=1)
    first = pl.multiple_of(3 * S * (1 - sx), S)
    side = dot(left, wc[:, pl.ds(first, 2 * S)]).reshape(H, 16, 2 * S)
    close = jnp.where(sx == 0, side[:, :, :S], side[:, :, S:])
    far = jnp.where(sx == 0, side[:, :, S:], side[:, :, :S])
    lane8 = lax.broadcasted_iota(jnp.int32, (1, 8, S), 1)
    outer = lane8 == 7 * (1 - sx)
    inner = lane8 == 5 * (1 - sx) + 1
    at = pl.multiple_of(8 * (1 - sx), 8)
    drive4 = drive.reshape(T, H, W, S)
    for f in range(T):
        add = jnp.where(outer, close[:, f:f + 1, :] + far[:, 4 + f:5 + f, :], 0.0)
        add = add + jnp.where(inner, far[:, f:f + 1, :], 0.0)
        drive4[f, :, pl.ds(at, 8), :] += add

    state = gain[0] * drive[0]
    for f in range(1, T):
        decay = loc[f]
        loc[f - 1] = state
        state = decay * state + gain[f] * drive[f]
    loc[T - 1] = state
    sb[...] = state.reshape(ROW, H, S)
    for p in peers:
        send(sb.at[p], rb.at[r], sems_b, p, r, {"tm": base + p}).start()
    rb[r] = sb[r]

    for p in peers:
        send(sa.at[p], ra.at[p], sems_a, p, p, {"tm": base + p}).wait()
    total_a = ra[0]
    for k in range(1, ROW):
        total_a = total_a * ra[k]
    ta[...] = total_a
    for c in columns:
        send(ta, ca.at[y], sems_ca, c, y, {"tm": c * ROW + r}).start()
    for c in w2loads:
        c.wait()

    for p in peers:
        send(sb.at[p], rb.at[p], sems_b, p, p, {"tm": base + p}).wait()
    total_b = rb[0]
    for k in range(1, ROW):
        total_b = ra[k] * total_b + rb[k]
    tb[...] = total_b
    for c in columns:
        send(tb, cb.at[y], sems_cb, c, y, {"tm": c * ROW + r}).start()
    for c in columns:
        send(ta, ca.at[c], sems_ca, c, c, {"tm": c * ROW + r}).wait()
    for c in columns:
        send(tb, cb.at[c], sems_cb, c, c, {"tm": c * ROW + r}).wait()
    ca[y] = total_a
    cb[y] = total_b
    carry = jnp.zeros_like(total_b)
    for c in range(cols):
        carry = jnp.where(c < y, ca[c] * carry + cb[c], carry)
    so[0] = carry
    for k in range(ROW - 1):
        carry = ra[k] * carry + rb[k]
        so[k + 1] = carry
    for p in peers:
        send(so.at[p], inc.at[r], sems_o, p, r, {"tm": base + p}).start()
    inc[r] = so[r]
    for p in peers:
        send(so.at[p], inc.at[p], sems_o, p, p, {"tm": base + p}).wait()

    before = inc[...].reshape(PIX, S)
    for f in range(T):
        state = loc[f] + fade[f] * before
        high = state.astype(BF16)
        low = (state - high.astype(F32)).astype(BF16)
        hid[f, pl.ds(1, H)] = jnp.concatenate([high, low], axis=1).reshape(H, W, C)
    edge = 15 * (1 - sx)
    target = jnp.where(slot < 4, slot * PIX + (row_id // 16) * W + edge, -1)
    picked = jnp.zeros((PIX, C), F32)
    for f in range(T):
        pick = jnp.where(lane + f * PIX == target, 1.0, 0.0).astype(BF16)
        picked = picked + dot(pick, hid[f, pl.ds(1, H)].reshape(PIX, C))
    sc2[...] = picked.astype(BF16).reshape(H, 16, C)
    halo_copies = [
        send(hid.at[:, pl.ds(1 + 15 * (1 - sy), 1)], hr2, halo2, 0, 0, near[0]),
        send(sc2, hc2.at[pl.ds(1, H)], halo2, 1, 1, near[1]),
        send(sc2.at[pl.ds(15 * (1 - sy), 1)], hc2.at[pl.ds(17 * sy, 1)], halo2, 2, 2, near[2]),
    ]
    for c in halo_copies:
        c.start()

    for f in range(T):
        left = jnp.concatenate([hid[f, pl.ds(dy, H)].reshape(PIX, C) for dy in range(3)], axis=1)
        direct = skip[...] * xp[f, pl.ds(2, H)].reshape(PIX, C).astype(F32)
        acc[f] = shifted(dot(left, wc2[...]), 3, C, 1) + direct

    for c in halo_copies:
        c.wait()
    first = pl.multiple_of(2 * C * (1 - sy), C)
    extra = shifted(dot(hr2[...].reshape(T * W, C), wc2[pl.ds(first, C), :]), 3, C, 1).reshape(T, W, C)
    at = pl.multiple_of(15 * W * (1 - sy), W)
    for f in range(T):
        acc[f, pl.ds(at, W), :] += extra[f]
    left = jnp.concatenate([hc2[pl.ds(dy, H)].reshape(PIX, C) for dy in range(3)], axis=1)
    first = pl.multiple_of(2 * C * (1 - sx), C)
    side = dot(left, wc2[:, pl.ds(first, C)]).reshape(H, 16, C)
    at = pl.multiple_of(8 * (1 - sx), 8)
    outer = lax.broadcasted_iota(jnp.int32, (1, 8, C), 1) == 7 * (1 - sx)
    acc4 = acc.reshape(T, H, W, C)
    for f in range(T):
        acc4[f, :, pl.ds(at, 8), :] += jnp.where(outer, side[:, f:f + 1, :], 0.0)
    for f in range(T):
        out[f] = acc[f].reshape(H, W, C).astype(BF16)


def body(frames, in_kernel, dt_weight, rates, out_kernel, skip):
    cols = lax.axis_size("tm") // ROW
    vmem = pl.BlockSpec(memory_space=pltpu.VMEM)
    hbm = pl.BlockSpec(memory_space=pl.ANY)

    def kernel(*refs):
        layer_kernel(cols, *refs)

    dma = pltpu.SemaphoreType.DMA
    chunk = (H, S)
    return pl.pallas_call(
        kernel,
        out_shape=jax.ShapeDtypeStruct(frames.shape, BF16),
        in_specs=[hbm, hbm, vmem, vmem, hbm, vmem],
        out_specs=vmem,
        scratch_shapes=[
            pltpu.VMEM((T, H + 4, W, C), BF16),
            pltpu.VMEM((5 * C, 5 * S), BF16),
            pltpu.VMEM((3 * C, 3 * C), BF16),
            pltpu.VMEM((T, 3, W, C), BF16),
            pltpu.VMEM((H + 4, 16, C), BF16),
            pltpu.VMEM((H, 16, C), BF16),
            pltpu.VMEM((T, PIX, S), F32),
            pltpu.VMEM((T, PIX, S), F32),
            pltpu.VMEM((T, PIX, S), F32),
            pltpu.VMEM((T, PIX, S), F32),
            pltpu.VMEM((T, H + 2, W, C), BF16),
            pltpu.VMEM((T, 1, W, C), BF16),
            pltpu.VMEM((H + 2, 16, C), BF16),
            pltpu.VMEM((H, 16, C), BF16),
            pltpu.VMEM((T, PIX, C), F32),
            pltpu.VMEM((ROW,) + chunk, F32),
            pltpu.VMEM((ROW,) + chunk, F32),
            pltpu.VMEM((ROW,) + chunk, F32),
            pltpu.VMEM((ROW,) + chunk, F32),
            pltpu.VMEM((cols,) + chunk, F32),
            pltpu.VMEM((cols,) + chunk, F32),
            pltpu.VMEM(chunk, F32),
            pltpu.VMEM(chunk, F32),
            pltpu.VMEM((ROW,) + chunk, F32),
            pltpu.VMEM((ROW,) + chunk, F32),
            dma,
            dma((25,)),
            dma((18,)),
            dma((2, 3)),
            dma((2, 3)),
            dma((2, ROW)),
            dma((2, ROW)),
            dma((2, cols)),
            dma((2, cols)),
            dma((2, ROW)),
        ],
        compiler_params=pltpu.CompilerParams(
            collective_id=0, has_side_effects=True, vmem_limit_bytes=48 * 1024 * 1024),
    )(frames, in_kernel.reshape(25, C, S), dt_weight, rates.reshape(1, S),
      out_kernel.reshape(9, S, C), skip.reshape(1, C))


def solution(mesh):
    return jax.shard_map(
        body,
        mesh=mesh,
        in_specs=(P("tm", "sy", "sx", None), P(), P(), P(), P(), P()),
        out_specs=P("tm", "sy", "sx", None),
        check_vma=False,
    )
```

```python
import jax
import jax.numpy as jnp
from jax import lax
from jax.experimental import pallas as pl
from jax.experimental.pallas import tpu as pltpu
from jax.sharding import PartitionSpec as P

ROW = 16
T, H, W = 4, 16, 16
PIX = H * W
C, S = 256, 128
MESH = pl.DeviceIdType.MESH
ORDER = [8, 7, 9, 6, 10, 5, 11, 4, 12, 3, 13, 2, 14, 1, 15]
F32 = jnp.float32
BF16 = jnp.bfloat16


def dot(a, b):
    return jnp.dot(a, b, preferred_element_type=F32)


def shifted(wide, taps, width, reach):
    rows = wide.shape[0]
    column = lax.rem(lax.broadcasted_iota(jnp.int32, (rows, width), 0), W)
    total = wide[:, reach * width:(reach + 1) * width]
    for tap in range(taps):
        move = tap - reach
        if move == 0:
            continue
        part = pltpu.roll(wide[:, tap * width:(tap + 1) * width], (-move) % rows, 0)
        inside = (column + move >= 0) & (column + move < W)
        total = total + jnp.where(inside, part, 0.0)
    return total


def one_minus_exp(u):
    series = u * (1.0 - u * (1 / 2) * (1.0 - u * (1 / 3) * (1.0 - u * (1 / 4) * (1.0 - u * (1 / 5) * (
        1.0 - u * (1 / 6) * (1.0 - u * (1 / 7) * (1.0 - u * (1 / 8))))))))
    return jnp.where(u < 0.5, series, 1.0 - jnp.exp(-u))


def layer_kernel(cols, frames, w1, dt, rates, w2, skip, out,
                 dts, spd, skp, carried, xp, wc, wc2, hr, hc, sc, gain, fade, drive, loc, hid, hr2, hc2, sc2, acc,
                 sa, sb, ra, rb, ca, cb, ta, tb, so, inc,
                 row_ready, col_ready, small, load, wload, w2load, halo, halo2, sems_a, sems_b, sems_ca, sems_cb, sems_o):
    me = lax.axis_index("tm")
    sy = lax.axis_index("sy")
    sx = lax.axis_index("sx")
    r = lax.rem(me, ROW)
    y = lax.div(me, ROW)
    base = me - r
    peers = [lax.rem(r + d, ROW) for d in ORDER]
    near = [{"sy": 1 - sy}, {"sx": 1 - sx}, {"sy": 1 - sy, "sx": 1 - sx}]

    loads = [pltpu.make_async_copy(frames, xp.at[:, pl.ds(2, H)], load)]
    loads[0].start()
    smalls = [pltpu.make_async_copy(dt, dts, small.at[0]), pltpu.make_async_copy(rates, spd, small.at[1]),
              pltpu.make_async_copy(skip, skp, small.at[2])]
    for c in smalls:
        c.start()
    wloads = []
    for i in range(25):
        wloads.append(pltpu.make_async_copy(
            w1.at[i], wc.at[pl.ds((i // 5) * C, C), pl.ds((i % 5) * S, S)], wload.at[i]))
    for c in wloads:
        c.start()
    w2loads = []
    for i in range(9):
        for half in range(2):
            w2loads.append(pltpu.make_async_copy(
                w2.at[i], wc2.at[pl.ds((i // 3) * C + half * S, S), pl.ds((i % 3) * C, C)],
                w2load.at[2 * i + half]))
    for c in w2loads:
        c.start()

    zrow = jnp.zeros((W, C), BF16)
    for f in range(T):
        for row in (0, 1, 18, 19):
            xp[f, row] = zrow
        hr[f, 2 * sy] = zrow
        hid[f, 0] = zrow
        hid[f, 17] = zrow
    for row in range(2):
        hc[18 * sy + row] = zrow
    hc2[17 * sy] = zrow

    barrier = pltpu.get_barrier_semaphore()
    for where in near:
        pl.semaphore_signal(barrier, inc=1, device_id=where, device_id_type=MESH)
    for p in range(ROW):
        @pl.when(p > r)
        def _(p=p):
            pl.semaphore_signal(barrier, inc=1, device_id={"tm": base + p}, device_id_type=MESH)
    for c in range(cols):
        @pl.when(c > y)
        def _(c=c):
            pl.semaphore_signal(barrier, inc=1, device_id={"tm": c * ROW + r}, device_id_type=MESH)

    loads[0].wait()
    row_id = lax.broadcasted_iota(jnp.int32, (PIX, 1), 0)
    slot = lax.rem(row_id, 16)
    edge = jnp.where(sx == 0, 15 - slot // 4, slot // 4)
    target = jnp.where(slot < 8, lax.rem(slot, 4) * PIX + (row_id // 16) * W + edge, -1)
    lane = lax.broadcasted_iota(jnp.int32, (PIX, PIX), 1)
    picked = jnp.zeros((PIX, C), F32)
    for f in range(T):
        pick = jnp.where(lane + f * PIX == target, 1.0, 0.0).astype(BF16)
        picked = picked + dot(pick, xp[f, pl.ds(2, H)].reshape(PIX, C))
    sc[...] = picked.astype(BF16).reshape(H, 16, C)

    def send(src, dst, sems, slot_out, slot_in, where):
        return pltpu.make_async_remote_copy(
            src_ref=src, dst_ref=dst, send_sem=sems.at[0, slot_out], recv_sem=sems.at[1, slot_in],
            device_id=where, device_id_type=MESH)

    pl.semaphore_wait(barrier, len(near) + r + y)
    for p in range(ROW):
        @pl.when(p < r)
        def _(p=p):
            pl.semaphore_signal(row_ready, inc=1, device_id={"tm": base + p}, device_id_type=MESH)
    for c in range(cols):
        @pl.when(c < y)
        def _(c=c):
            pl.semaphore_signal(col_ready, inc=1, device_id={"tm": c * ROW + r}, device_id_type=MESH)
    halo_copies = [
        send(frames.at[:, pl.ds(14 * (1 - sy), 2)], hr.at[:, pl.ds(sy, 2)], halo, 0, 0, near[0]),
        send(sc, hc.at[pl.ds(2, H)], halo, 1, 1, near[1]),
        send(sc.at[pl.ds(14 * (1 - sy), 2)], hc.at[pl.ds(18 * sy, 2)], halo, 2, 2, near[2]),
    ]
    for c in halo_copies:
        c.start()

    for c in smalls:
        c.wait()
    weight = jnp.broadcast_to(dts[...].reshape(1, C), (S, C))
    speed = spd[...]
    faded = None
    for f in range(T):
        v = lax.dot_general(xp[f, pl.ds(2, H)].reshape(PIX, C), weight, (((1,), (1,)), ((), ())),
                            preferred_element_type=F32)
        scaled = (jnp.maximum(v, 0.0) + jnp.log1p(jnp.exp(-jnp.abs(v)))) * speed
        decay = jnp.exp(-scaled)
        gain[f] = jnp.sqrt(one_minus_exp(2.0 * scaled))
        loc[f] = decay
        faded = decay if f == 0 else faded * decay
        fade[f] = faded
    sa[...] = faded.reshape(ROW, H, S)
    ra[r] = sa[r]

    for c in wloads:
        c.wait()
    for f in range(T):
        left = jnp.concatenate([xp[f, pl.ds(dy, H)].reshape(PIX, C) for dy in range(5)], axis=1)
        drive[f] = shifted(dot(left, wc[...]), 5, S, 2)
    @pl.when(r < ROW - 1)
    def _():
        pl.semaphore_wait(row_ready, ROW - 1 - r)
    for p in peers:
        send(sa.at[p], ra.at[r], sems_a, p, r, {"tm": base + p}).start()

    for c in halo_copies:
        c.wait()
    left = jnp.concatenate([hr[:, pl.ds(k, 2)].reshape(T * 2 * W, C) for k in range(2)], axis=1)
    first = pl.multiple_of(3 * C * (1 - sy), C)
    extra = shifted(dot(left, wc[pl.ds(first, 2 * C), :]), 5, S, 2).reshape(T, 2 * W, S)
    at = pl.multiple_of(14 * W * (1 - sy), 2 * W)
    for f in range(T):
        drive[f, pl.ds(at, 2 * W), :] += extra[f]
    left = jnp.concatenate([hc[pl.ds(dy, H)].reshape(PIX, C) for dy in range(5)], axis=1)
    first = pl.multiple_of(3 * S * (1 - sx), S)
    side = dot(left, wc[:, pl.ds(first, 2 * S)]).reshape(H, 16, 2 * S)
    close = jnp.where(sx == 0, side[:, :, :S], side[:, :, S:])
    far = jnp.where(sx == 0, side[:, :, S:], side[:, :, :S])
    lane8 = lax.broadcasted_iota(jnp.int32, (1, 8, S), 1)
    outer = lane8 == 7 * (1 - sx)
    inner = lane8 == 5 * (1 - sx) + 1
    at = pl.multiple_of(8 * (1 - sx), 8)
    drive4 = drive.reshape(T, H, W, S)
    for f in range(T):
        add = jnp.where(outer, close[:, f:f + 1, :] + far[:, 4 + f:5 + f, :], 0.0)
        add = add + jnp.where(inner, far[:, f:f + 1, :], 0.0)
        drive4[f, :, pl.ds(at, 8), :] += add

    state = gain[0] * drive[0]
    for f in range(1, T):
        decay = loc[f]
        loc[f - 1] = state
        state = decay * state + gain[f] * drive[f]
    loc[T - 1] = state
    sb[...] = state.reshape(ROW, H, S)
    for p in peers:
        send(sb.at[p], rb.at[r], sems_b, p, r, {"tm": base + p}).start()
    rb[r] = sb[r]

    for p in peers:
        send(sa.at[p], ra.at[p], sems_a, p, p, {"tm": base + p}).wait()
    total_a = ra[0]
    for k in range(1, ROW):
        total_a = total_a * ra[k]
    ta[...] = total_a
    @pl.when(y < cols - 1)
    def _():
        pl.semaphore_wait(col_ready, cols - 1 - y)
    for c in range(cols):
        @pl.when(c > y)
        def _(c=c):
            send(ta, ca.at[y], sems_ca, c, y, {"tm": c * ROW + r}).start()
    for c in w2loads:
        c.wait()

    for p in peers:
        send(sb.at[p], rb.at[p], sems_b, p, p, {"tm": base + p}).wait()
    total_b = rb[0]
    for k in range(1, ROW):
        total_b = ra[k] * total_b + rb[k]
    tb[...] = total_b
    for c in range(cols):
        @pl.when(c > y)
        def _(c=c):
            send(tb, cb.at[y], sems_cb, c, y, {"tm": c * ROW + r}).start()
    carried[...] = jnp.zeros_like(total_b)
    for c in range(cols):
        @pl.when(c < y)
        def _(c=c):
            send(ta, ca.at[c], sems_ca, c, c, {"tm": c * ROW + r}).wait_recv()
            send(tb, cb.at[c], sems_cb, c, c, {"tm": c * ROW + r}).wait_recv()
            carried[...] = ca[c] * carried[...] + cb[c]
    carry = carried[...]
    so[0] = carry
    for k in range(ROW - 1):
        carry = ra[k] * carry + rb[k]
        so[k + 1] = carry
    for p in peers:
        send(so.at[p], inc.at[r], sems_o, p, r, {"tm": base + p}).start()
    inc[r] = so[r]
    for p in peers:
        send(so.at[p], inc.at[p], sems_o, p, p, {"tm": base + p}).wait()

    for c in range(cols):
        @pl.when(c > y)
        def _(c=c):
            send(ta, ca.at[y], sems_ca, c, y, {"tm": c * ROW + r}).wait_send()
            send(tb, cb.at[y], sems_cb, c, y, {"tm": c * ROW + r}).wait_send()

    before = inc[...].reshape(PIX, S)
    for f in range(T):
        state = loc[f] + fade[f] * before
        high = state.astype(BF16)
        low = (state - high.astype(F32)).astype(BF16)
        hid[f, pl.ds(1, H)] = jnp.concatenate([high, low], axis=1).reshape(H, W, C)
    edge = 15 * (1 - sx)
    target = jnp.where(slot < 4, slot * PIX + (row_id // 16) * W + edge, -1)
    picked = jnp.zeros((PIX, C), F32)
    for f in range(T):
        pick = jnp.where(lane + f * PIX == target, 1.0, 0.0).astype(BF16)
        picked = picked + dot(pick, hid[f, pl.ds(1, H)].reshape(PIX, C))
    sc2[...] = picked.astype(BF16).reshape(H, 16, C)
    halo_copies = [
        send(hid.at[:, pl.ds(1 + 15 * (1 - sy), 1)], hr2, halo2, 0, 0, near[0]),
        send(sc2, hc2.at[pl.ds(1, H)], halo2, 1, 1, near[1]),
        send(sc2.at[pl.ds(15 * (1 - sy), 1)], hc2.at[pl.ds(17 * sy, 1)], halo2, 2, 2, near[2]),
    ]
    for c in halo_copies:
        c.start()

    for f in range(T):
        left = jnp.concatenate([hid[f, pl.ds(dy, H)].reshape(PIX, C) for dy in range(3)], axis=1)
        direct = skp[...] * xp[f, pl.ds(2, H)].reshape(PIX, C).astype(F32)
        acc[f] = shifted(dot(left, wc2[...]), 3, C, 1) + direct

    for c in halo_copies:
        c.wait()
    first = pl.multiple_of(2 * C * (1 - sy), C)
    extra = shifted(dot(hr2[...].reshape(T * W, C), wc2[pl.ds(first, C), :]), 3, C, 1).reshape(T, W, C)
    at = pl.multiple_of(15 * W * (1 - sy), W)
    for f in range(T):
        acc[f, pl.ds(at, W), :] += extra[f]
    left = jnp.concatenate([hc2[pl.ds(dy, H)].reshape(PIX, C) for dy in range(3)], axis=1)
    first = pl.multiple_of(2 * C * (1 - sx), C)
    side = dot(left, wc2[:, pl.ds(first, C)]).reshape(H, 16, C)
    at = pl.multiple_of(8 * (1 - sx), 8)
    outer = lax.broadcasted_iota(jnp.int32, (1, 8, C), 1) == 7 * (1 - sx)
    acc4 = acc.reshape(T, H, W, C)
    for f in range(T):
        acc4[f, :, pl.ds(at, 8), :] += jnp.where(outer, side[:, f:f + 1, :], 0.0)
    for f in range(T):
        out[f] = acc[f].reshape(H, W, C).astype(BF16)


def body(frames, in_kernel, dt_weight, rates, out_kernel, skip):
    cols = lax.axis_size("tm") // ROW
    vmem = pl.BlockSpec(memory_space=pltpu.VMEM)
    hbm = pl.BlockSpec(memory_space=pltpu.HBM)

    def kernel(*refs):
        layer_kernel(cols, *refs)

    dma = pltpu.SemaphoreType.DMA
    chunk = (H, S)
    return pl.pallas_call(
        kernel,
        out_shape=jax.ShapeDtypeStruct(frames.shape, BF16),
        in_specs=[hbm] * 6,
        out_specs=vmem,
        scratch_shapes=[
            pltpu.VMEM((C,), BF16),
            pltpu.VMEM((1, S), F32),
            pltpu.VMEM((1, C), F32),
            pltpu.VMEM(chunk, F32),
            pltpu.VMEM((T, H + 4, W, C), BF16),
            pltpu.VMEM((5 * C, 5 * S), BF16),
            pltpu.VMEM((3 * C, 3 * C), BF16),
            pltpu.VMEM((T, 3, W, C), BF16),
            pltpu.VMEM((H + 4, 16, C), BF16),
            pltpu.VMEM((H, 16, C), BF16),
            pltpu.VMEM((T, PIX, S), F32),
            pltpu.VMEM((T, PIX, S), F32),
            pltpu.VMEM((T, PIX, S), F32),
            pltpu.VMEM((T, PIX, S), F32),
            pltpu.VMEM((T, H + 2, W, C), BF16),
            pltpu.VMEM((T, 1, W, C), BF16),
            pltpu.VMEM((H + 2, 16, C), BF16),
            pltpu.VMEM((H, 16, C), BF16),
            pltpu.VMEM((T, PIX, C), F32),
            pltpu.VMEM((ROW,) + chunk, F32),
            pltpu.VMEM((ROW,) + chunk, F32),
            pltpu.VMEM((ROW,) + chunk, F32),
            pltpu.VMEM((ROW,) + chunk, F32),
            pltpu.VMEM((cols,) + chunk, F32),
            pltpu.VMEM((cols,) + chunk, F32),
            pltpu.VMEM(chunk, F32),
            pltpu.VMEM(chunk, F32),
            pltpu.VMEM((ROW,) + chunk, F32),
            pltpu.VMEM((ROW,) + chunk, F32),
            pltpu.SemaphoreType.REGULAR,
            pltpu.SemaphoreType.REGULAR,
            dma((3,)),
            dma,
            dma((25,)),
            dma((18,)),
            dma((2, 3)),
            dma((2, 3)),
            dma((2, ROW)),
            dma((2, ROW)),
            dma((2, cols)),
            dma((2, cols)),
            dma((2, ROW)),
        ],
        compiler_params=pltpu.CompilerParams(
            collective_id=0, has_side_effects=True, vmem_limit_bytes=67_000_000),
    )(frames, in_kernel.reshape(25, C, S), dt_weight, rates.reshape(1, S),
      out_kernel.reshape(9, S, C), skip.reshape(1, C))


def solution(mesh):
    return jax.shard_map(
        body,
        mesh=mesh,
        in_specs=(P("tm", "sy", "sx", None), P(), P(), P(), P(), P()),
        out_specs=P("tm", "sy", "sx", None),
        check_vma=False,
    )
```

```python
import jax
import jax.numpy as jnp
from jax import lax
from jax.experimental import pallas as pl
from jax.experimental.pallas import tpu as pltpu
from jax.sharding import PartitionSpec as P

ROW = 16
T, H, W = 4, 16, 16
PIX = H * W
C, S = 256, 128
MESH = pl.DeviceIdType.MESH
ORDER = [8, 7, 9, 6, 10, 5, 11, 4, 12, 3, 13, 2, 14, 1, 15]
F32 = jnp.float32
BF16 = jnp.bfloat16


def dot(a, b):
    return jnp.dot(a, b, preferred_element_type=F32)


def shifted(wide, taps, width, reach):
    rows = wide.shape[0]
    column = lax.rem(lax.broadcasted_iota(jnp.int32, (rows, width), 0), W)
    total = wide[:, reach * width:(reach + 1) * width]
    for tap in range(taps):
        move = tap - reach
        if move == 0:
            continue
        part = pltpu.roll(wide[:, tap * width:(tap + 1) * width], (-move) % rows, 0)
        inside = (column + move >= 0) & (column + move < W)
        total = total + jnp.where(inside, part, 0.0)
    return total


def one_minus_exp(u):
    series = u * (1.0 - u * (1 / 2) * (1.0 - u * (1 / 3) * (1.0 - u * (1 / 4) * (1.0 - u * (1 / 5) * (
        1.0 - u * (1 / 6) * (1.0 - u * (1 / 7) * (1.0 - u * (1 / 8))))))))
    return jnp.where(u < 0.5, series, 1.0 - jnp.exp(-u))


def layer_kernel(cols, frames, w1, dt, rates, w2, skip, out,
                 dts, spd, skp, carried, xp, wc, wc2, hr, hc, sc, gain, fade, drive, loc, hid, hr2, hc2, acc, er, ec, ner, nec, se, ie, ir,
                 sa, sb, ra, rb, ca, cb, ta, tb, so, inc,
                 row_ready, col_ready, tile_ready, small, load, wload, w2load, halo, halo2, sems_a, sems_b, sems_ca, sems_cb, sems_o, sems_e, sems_r, sems_c):
    me = lax.axis_index("tm")
    sy = lax.axis_index("sy")
    sx = lax.axis_index("sx")
    r = lax.rem(me, ROW)
    y = lax.div(me, ROW)
    base = me - r
    peers = [lax.rem(r + d, ROW) for d in ORDER]
    near = [{"sy": 1 - sy}, {"sx": 1 - sx}, {"sy": 1 - sy, "sx": 1 - sx}]

    loads = [pltpu.make_async_copy(frames, xp.at[:, pl.ds(2, H)], load)]
    loads[0].start()
    smalls = [pltpu.make_async_copy(dt, dts, small.at[0]), pltpu.make_async_copy(rates, spd, small.at[1]),
              pltpu.make_async_copy(skip, skp, small.at[2])]
    for c in smalls:
        c.start()
    wloads = []
    for i in range(25):
        wloads.append(pltpu.make_async_copy(
            w1.at[i], wc.at[pl.ds((i // 5) * C, C), pl.ds((i % 5) * S, S)], wload.at[i]))
    for c in wloads:
        c.start()
    w2loads = []
    for i in range(9):
        for half in range(2):
            w2loads.append(pltpu.make_async_copy(
                w2.at[i], wc2.at[pl.ds((i // 3) * C + half * S, S), pl.ds((i % 3) * C, C)],
                w2load.at[2 * i + half]))
    for c in w2loads:
        c.start()

    zrow = jnp.zeros((W, C), BF16)
    for f in range(T):
        for row in (0, 1, 18, 19):
            xp[f, row] = zrow
        hr[f, 2 * sy] = zrow
        hid[f, 0] = zrow
        hid[f, 17] = zrow
    for row in range(2):
        hc[18 * sy + row] = zrow[:8]
    nec[17 * sy] = jnp.zeros((8, S), F32)
    ie[17 * sy] = jnp.zeros((1, S), F32)

    barrier = pltpu.get_barrier_semaphore()
    for where in near:
        pl.semaphore_signal(barrier, inc=1, device_id=where, device_id_type=MESH)
    for p in range(ROW):
        @pl.when(p > r)
        def _(p=p):
            pl.semaphore_signal(barrier, inc=1, device_id={"tm": base + p}, device_id_type=MESH)
    for c in range(cols):
        @pl.when(c > y)
        def _(c=c):
            pl.semaphore_signal(barrier, inc=1, device_id={"tm": c * ROW + r}, device_id_type=MESH)

    loads[0].wait()
    row_id = lax.broadcasted_iota(jnp.int32, (8 * H, 1), 0)
    slot = lax.rem(row_id, 8)
    edge = jnp.where(sx == 0, 15 - slot // 4, slot // 4)
    target = lax.rem(slot, 4) * PIX + (row_id // 8) * W + edge
    lane = lax.broadcasted_iota(jnp.int32, (8 * H, PIX), 1)
    picked = jnp.zeros((8 * H, C), F32)
    for f in range(T):
        pick = jnp.where(lane + f * PIX == target, 1.0, 0.0).astype(BF16)
        picked = picked + dot(pick, xp[f, pl.ds(2, H)].reshape(PIX, C))
    sc[...] = picked.astype(BF16).reshape(H, 8, C)

    def send(src, dst, sems, slot_out, slot_in, where):
        return pltpu.make_async_remote_copy(
            src_ref=src, dst_ref=dst, send_sem=sems.at[0, slot_out], recv_sem=sems.at[1, slot_in],
            device_id=where, device_id_type=MESH)

    pl.semaphore_wait(barrier, len(near) + r + y)
    for p in range(ROW):
        @pl.when(p < r)
        def _(p=p):
            pl.semaphore_signal(row_ready, inc=1, device_id={"tm": base + p}, device_id_type=MESH)
    for c in range(cols):
        @pl.when(c < y)
        def _(c=c):
            pl.semaphore_signal(col_ready, inc=1, device_id={"tm": c * ROW + r}, device_id_type=MESH)
    halo_copies = [
        send(frames.at[:, pl.ds(14 * (1 - sy), 2)], hr.at[:, pl.ds(sy, 2)], halo, 0, 0, near[0]),
        send(sc, hc.at[pl.ds(2, H)], halo, 1, 1, near[1]),
        send(sc.at[pl.ds(14 * (1 - sy), 2)], hc.at[pl.ds(18 * sy, 2)], halo, 2, 2, near[2]),
    ]
    for c in halo_copies:
        c.start()

    for c in smalls:
        c.wait()
    weight = jnp.broadcast_to(dts[...].reshape(1, C), (S, C))
    speed = spd[...]
    faded = None
    for f in range(T):
        v = lax.dot_general(xp[f, pl.ds(2, H)].reshape(PIX, C), weight, (((1,), (1,)), ((), ())),
                            preferred_element_type=F32)
        scaled = (jnp.maximum(v, 0.0) + jnp.log1p(jnp.exp(-jnp.abs(v)))) * speed
        decay = jnp.exp(-scaled)
        gain[f] = jnp.sqrt(one_minus_exp(2.0 * scaled))
        loc[f] = decay
        faded = decay if f == 0 else faded * decay
        fade[f] = faded
    sa[...] = faded.reshape(ROW, H, S)
    ra[r] = sa[r]

    for c in wloads:
        c.wait()
    for f in range(T):
        left = jnp.concatenate([xp[f, pl.ds(dy, H)].reshape(PIX, C) for dy in range(5)], axis=1)
        drive[f] = shifted(dot(left, wc[...]), 5, S, 2)
    @pl.when(r < ROW - 1)
    def _():
        pl.semaphore_wait(row_ready, ROW - 1 - r)
    for p in peers:
        send(sa.at[p], ra.at[r], sems_a, p, r, {"tm": base + p}).start()

    for c in halo_copies:
        c.wait()
    left = jnp.concatenate([hr[:, pl.ds(k, 2)].reshape(T * 2 * W, C) for k in range(2)], axis=1)
    first = pl.multiple_of(3 * C * (1 - sy), C)
    extra = shifted(dot(left, wc[pl.ds(first, 2 * C), :]), 5, S, 2).reshape(T, 2 * W, S)
    at = pl.multiple_of(14 * W * (1 - sy), 2 * W)
    for f in range(T):
        drive[f, pl.ds(at, 2 * W), :] += extra[f]
    left = jnp.concatenate([hc[pl.ds(dy, H)].reshape(8 * H, C) for dy in range(5)], axis=1)
    first = pl.multiple_of(3 * S * (1 - sx), S)
    side = dot(left, wc[:, pl.ds(first, 2 * S)]).reshape(H, 8, 2 * S)
    close = jnp.where(sx == 0, side[:, :, :S], side[:, :, S:])
    far = jnp.where(sx == 0, side[:, :, S:], side[:, :, :S])
    lane8 = lax.broadcasted_iota(jnp.int32, (1, 8, S), 1)
    outer = lane8 == 7 * (1 - sx)
    inner = lane8 == 5 * (1 - sx) + 1
    at = pl.multiple_of(8 * (1 - sx), 8)
    drive4 = drive.reshape(T, H, W, S)
    for f in range(T):
        add = jnp.where(outer, close[:, f:f + 1, :] + far[:, 4 + f:5 + f, :], 0.0)
        add = add + jnp.where(inner, far[:, f:f + 1, :], 0.0)
        drive4[f, :, pl.ds(at, 8), :] += add

    state = gain[0] * drive[0]
    for f in range(1, T):
        decay = loc[f]
        loc[f - 1] = state
        state = decay * state + gain[f] * drive[f]
    loc[T - 1] = state
    sb[...] = state.reshape(ROW, H, S)
    for p in peers:
        send(sb.at[p], rb.at[r], sems_b, p, r, {"tm": base + p}).start()
    rb[r] = sb[r]

    for where in near:
        pl.semaphore_signal(tile_ready, inc=1, device_id=where, device_id_type=MESH)
    edge_row = pl.multiple_of(15 * W * (1 - sy), W)
    edge_x = 15 * (1 - sx)
    at_edge = lax.broadcasted_iota(jnp.int32, (1, W, S), 1) == edge_x
    ends = []
    for ref in (loc, fade):
        for f in range(T):
            ends.append(jnp.sum(jnp.where(at_edge, ref[f].reshape(H, W, S), 0.0), axis=1, keepdims=True))
    ec[...] = jnp.concatenate(ends, axis=1)
    for f in range(T):
        er[f] = loc[f, pl.ds(edge_row, W), :]
        er[T + f] = fade[f, pl.ds(edge_row, W), :]
    edge_copies = [
        send(er, ner, halo2, 0, 0, near[0]),
        send(ec, nec.at[pl.ds(1, H)], halo2, 1, 1, near[1]),
        send(ec.at[pl.ds(15 * (1 - sy), 1)], nec.at[pl.ds(17 * sy, 1)], halo2, 2, 2, near[2]),
    ]
    for c in edge_copies:
        c.start()

    for p in peers:
        send(sa.at[p], ra.at[p], sems_a, p, p, {"tm": base + p}).wait()
    total_a = ra[0]
    for k in range(1, ROW):
        total_a = total_a * ra[k]
    ta[...] = total_a
    @pl.when(y < cols - 1)
    def _():
        pl.semaphore_wait(col_ready, cols - 1 - y)
    for c in range(cols):
        @pl.when(c > y)
        def _(c=c):
            send(ta, ca.at[y], sems_ca, c, y, {"tm": c * ROW + r}).start()
    for c in w2loads:
        c.wait()

    for p in peers:
        send(sb.at[p], rb.at[p], sems_b, p, p, {"tm": base + p}).wait()
    total_b = rb[0]
    for k in range(1, ROW):
        total_b = ra[k] * total_b + rb[k]
    tb[...] = total_b
    for c in range(cols):
        @pl.when(c > y)
        def _(c=c):
            send(tb, cb.at[y], sems_cb, c, y, {"tm": c * ROW + r}).start()
    carried[...] = jnp.zeros_like(total_b)
    for c in range(cols):
        @pl.when(c < y)
        def _(c=c):
            send(ta, ca.at[c], sems_ca, c, c, {"tm": c * ROW + r}).wait_recv()
            send(tb, cb.at[c], sems_cb, c, c, {"tm": c * ROW + r}).wait_recv()
            carried[...] = ca[c] * carried[...] + cb[c]
    carry = carried[...]
    so[0] = carry
    for k in range(ROW - 1):
        carry = ra[k] * carry + rb[k]
        so[k + 1] = carry
    for p in peers:
        send(so.at[p], inc.at[r], sems_o, p, r, {"tm": base + p}).start()
    inc[r] = so[r]
    for k in range(ROW):
        se[k] = jnp.sum(jnp.where(at_edge[0], so[k], 0.0), axis=0, keepdims=True)
    pl.semaphore_wait(tile_ready, len(near))
    everyone = [r] + peers

    def to_column(p):
        return send(se.at[pl.ds(p, 1)], ie.at[pl.ds(1 + r, 1)], sems_e, p, r, {"tm": base + p, "sx": 1 - sx})

    def to_row(p):
        return send(so.at[p], ir, sems_r, p, 0, {"tm": base + p, "sy": 1 - sy})

    def to_corner(p):
        return send(se.at[pl.ds(p, 1)], ie.at[pl.ds(17 * sy, 1)], sems_c, p, 0,
                    {"tm": base + p, "sy": 1 - sy, "sx": 1 - sx})

    @pl.when(r == 15 * (1 - sy))
    def _():
        for p in everyone:
            to_row(p).start()
            to_corner(p).start()
    for p in everyone:
        to_column(p).start()
    for p in peers:
        send(so.at[p], inc.at[p], sems_o, p, p, {"tm": base + p}).wait()

    for c in range(cols):
        @pl.when(c > y)
        def _(c=c):
            send(ta, ca.at[y], sems_ca, c, y, {"tm": c * ROW + r}).wait_send()
            send(tb, cb.at[y], sems_cb, c, y, {"tm": c * ROW + r}).wait_send()

    before = inc[...].reshape(PIX, S)
    for f in range(T):
        state = loc[f] + fade[f] * before
        high = state.astype(BF16)
        low = (state - high.astype(F32)).astype(BF16)
        hid[f, pl.ds(1, H)] = jnp.concatenate([high, low], axis=1).reshape(H, W, C)

    for f in range(T):
        left = jnp.concatenate([hid[f, pl.ds(dy, H)].reshape(PIX, C) for dy in range(3)], axis=1)
        direct = skp[...] * xp[f, pl.ds(2, H)].reshape(PIX, C).astype(F32)
        acc[f] = shifted(dot(left, wc2[...]), 3, C, 1) + direct

    for c in edge_copies:
        c.wait()
    for p in everyone:
        send(se.at[pl.ds(p, 1)], ie.at[pl.ds(1 + p, 1)], sems_e, p, p, {"tm": base + p, "sx": 1 - sx}).wait()
    to_row(r).wait_recv()
    to_corner(r).wait_recv()

    @pl.when(r == 15 * (1 - sy))
    def _():
        for p in everyone:
            to_row(p).wait_send()
            to_corner(p).wait_send()
    state = ner[pl.ds(0, T)] + ner[pl.ds(T, T)] * ir[...].reshape(1, W, S)
    high = state.astype(BF16)
    hr2[...] = jnp.concatenate([high, (state - high.astype(F32)).astype(BF16)], axis=2)
    both = nec[...]
    state = both[:, :T] + both[:, T:] * ie[...]
    there = lax.broadcasted_iota(jnp.int32, (H + 2, 1, 1), 0) != 17 * sy
    state = jnp.where(there, state, 0.0)
    state = jnp.concatenate([state, jnp.zeros_like(state)], axis=1)
    high = state.astype(BF16)
    hc2[...] = jnp.concatenate([high, (state - high.astype(F32)).astype(BF16)], axis=2)
    first = pl.multiple_of(2 * C * (1 - sy), C)
    extra = shifted(dot(hr2[...].reshape(T * W, C), wc2[pl.ds(first, C), :]), 3, C, 1).reshape(T, W, C)
    at = pl.multiple_of(15 * W * (1 - sy), W)
    for f in range(T):
        acc[f, pl.ds(at, W), :] += extra[f]
    left = jnp.concatenate([hc2[pl.ds(dy, H)].reshape(8 * H, C) for dy in range(3)], axis=1)
    first = pl.multiple_of(2 * C * (1 - sx), C)
    side = dot(left, wc2[:, pl.ds(first, C)]).reshape(H, 8, C)
    at = pl.multiple_of(8 * (1 - sx), 8)
    outer = lax.broadcasted_iota(jnp.int32, (1, 8, C), 1) == 7 * (1 - sx)
    acc4 = acc.reshape(T, H, W, C)
    for f in range(T):
        acc4[f, :, pl.ds(at, 8), :] += jnp.where(outer, side[:, f:f + 1, :], 0.0)
    for f in range(T):
        out[f] = acc[f].reshape(H, W, C).astype(BF16)


def body(frames, in_kernel, dt_weight, rates, out_kernel, skip):
    cols = lax.axis_size("tm") // ROW
    vmem = pl.BlockSpec(memory_space=pltpu.VMEM)
    hbm = pl.BlockSpec(memory_space=pltpu.HBM)

    def kernel(*refs):
        layer_kernel(cols, *refs)

    dma = pltpu.SemaphoreType.DMA
    chunk = (H, S)
    return pl.pallas_call(
        kernel,
        out_shape=jax.ShapeDtypeStruct(frames.shape, BF16),
        in_specs=[hbm] * 6,
        out_specs=vmem,
        scratch_shapes=[
            pltpu.VMEM((C,), BF16),
            pltpu.VMEM((1, S), F32),
            pltpu.VMEM((1, C), F32),
            pltpu.VMEM(chunk, F32),
            pltpu.VMEM((T, H + 4, W, C), BF16),
            pltpu.VMEM((5 * C, 5 * S), BF16),
            pltpu.VMEM((3 * C, 3 * C), BF16),
            pltpu.VMEM((T, 3, W, C), BF16),
            pltpu.VMEM((H + 4, 8, C), BF16),
            pltpu.VMEM((H, 8, C), BF16),
            pltpu.VMEM((T, PIX, S), F32),
            pltpu.VMEM((T, PIX, S), F32),
            pltpu.VMEM((T, PIX, S), F32),
            pltpu.VMEM((T, PIX, S), F32),
            pltpu.VMEM((T, H + 2, W, C), BF16),
            pltpu.VMEM((T, W, C), BF16),
            pltpu.VMEM((H + 2, 8, C), BF16),
            pltpu.VMEM((T, PIX, C), F32),
            pltpu.VMEM((2 * T, W, S), F32),
            pltpu.VMEM((H, 2 * T, S), F32),
            pltpu.VMEM((2 * T, W, S), F32),
            pltpu.VMEM((H + 2, 2 * T, S), F32),
            pltpu.VMEM((ROW, 1, S), F32),
            pltpu.VMEM((H + 2, 1, S), F32),
            pltpu.VMEM(chunk, F32),
            pltpu.VMEM((ROW,) + chunk, F32),
            pltpu.VMEM((ROW,) + chunk, F32),
            pltpu.VMEM((ROW,) + chunk, F32),
            pltpu.VMEM((ROW,) + chunk, F32),
            pltpu.VMEM((cols,) + chunk, F32),
            pltpu.VMEM((cols,) + chunk, F32),
            pltpu.VMEM(chunk, F32),
            pltpu.VMEM(chunk, F32),
            pltpu.VMEM((ROW,) + chunk, F32),
            pltpu.VMEM((ROW,) + chunk, F32),
            pltpu.SemaphoreType.REGULAR,
            pltpu.SemaphoreType.REGULAR,
            pltpu.SemaphoreType.REGULAR,
            dma((3,)),
            dma,
            dma((25,)),
            dma((18,)),
            dma((2, 3)),
            dma((2, 3)),
            dma((2, ROW)),
            dma((2, ROW)),
            dma((2, cols)),
            dma((2, cols)),
            dma((2, ROW)),
            dma((2, ROW)),
            dma((2, ROW)),
            dma((2, ROW)),
        ],
        compiler_params=pltpu.CompilerParams(
            collective_id=0, has_side_effects=True, vmem_limit_bytes=67_000_000),
    )(frames, in_kernel.reshape(25, C, S), dt_weight, rates.reshape(1, S),
      out_kernel.reshape(9, S, C), skip.reshape(1, C))


def solution(mesh):
    return jax.shard_map(
        body,
        mesh=mesh,
        in_specs=(P("tm", "sy", "sx", None), P(), P(), P(), P(), P()),
        out_specs=P("tm", "sy", "sx", None),
        check_vma=False,
    )
```

```python
import jax
import jax.numpy as jnp
from jax import lax
from jax.experimental import pallas as pl
from jax.experimental.pallas import tpu as pltpu
from jax.sharding import PartitionSpec as P

ROW = 16
T, H, W = 4, 16, 16
PIX = H * W
C, S = 256, 128
MESH = pl.DeviceIdType.MESH
ORDER = [8, 7, 9, 6, 10, 5, 11, 4, 12, 3, 13, 2, 14, 1, 15]
F32 = jnp.float32
BF16 = jnp.bfloat16


def dot(a, b):
    return jnp.dot(a, b, preferred_element_type=F32)


def shifted(wide, taps, width, reach):
    rows = wide.shape[0]
    column = lax.rem(lax.broadcasted_iota(jnp.int32, (rows, width), 0), W)
    total = wide[:, reach * width:(reach + 1) * width]
    for tap in range(taps):
        move = tap - reach
        if move == 0:
            continue
        part = pltpu.roll(wide[:, tap * width:(tap + 1) * width], (-move) % rows, 0)
        inside = (column + move >= 0) & (column + move < W)
        total = total + jnp.where(inside, part, 0.0)
    return total


def one_minus_exp(u):
    series = u * (1.0 - u * (1 / 2) * (1.0 - u * (1 / 3) * (1.0 - u * (1 / 4) * (1.0 - u * (1 / 5) * (
        1.0 - u * (1 / 6) * (1.0 - u * (1 / 7) * (1.0 - u * (1 / 8))))))))
    return jnp.where(u < 0.5, series, 1.0 - jnp.exp(-u))


def layer_kernel(cols, frames, w1, dt, rates, w2, skip, out,
                 dts, spd, skp, carried, xp, wc, wc2, hr, hc, sc, gain, fade, keep, loc, hid, hr2, hc2, acc, done, er, ec, ner, nec, se, ie, ir,
                 sa, sb, ra, rb, ca, cb, ta, tb, so, inc,
                 row_ready, col_ready, tile_ready, small, store, load, wload, w2load, halo, halo2, sems_a, sems_b, sems_ca, sems_cb, sems_o, sems_e, sems_r, sems_c):
    me = lax.axis_index("tm")
    sy = lax.axis_index("sy")
    sx = lax.axis_index("sx")
    r = lax.rem(me, ROW)
    y = lax.div(me, ROW)
    base = me - r
    peers = [lax.rem(r + d, ROW) for d in ORDER]
    near = [{"sy": 1 - sy}, {"sx": 1 - sx}, {"sy": 1 - sy, "sx": 1 - sx}]

    zrow = jnp.zeros((W, C), BF16)
    for f in range(T):
        for row in (0, 1, 18, 19):
            xp[f, row] = zrow
        hr[f, 2 * sy] = zrow
        hid[f, 0] = zrow
        hid[f, 17] = zrow
    for row in range(2):
        hc[18 * sy + row] = zrow[:8]
    nec[17 * sy] = jnp.zeros((8, S), F32)
    ie[17 * sy] = jnp.zeros((1, S), F32)

    barrier = pltpu.get_barrier_semaphore()
    for where in near:
        pl.semaphore_signal(barrier, inc=1, device_id=where, device_id_type=MESH)
    for p in range(ROW):
        @pl.when(p > r)
        def _(p=p):
            pl.semaphore_signal(barrier, inc=1, device_id={"tm": base + p}, device_id_type=MESH)
    for c in range(cols):
        @pl.when(c > y)
        def _(c=c):
            pl.semaphore_signal(barrier, inc=1, device_id={"tm": c * ROW + r}, device_id_type=MESH)

    loads = [pltpu.make_async_copy(frames, xp.at[:, pl.ds(2, H)], load)]
    loads[0].start()
    smalls = [pltpu.make_async_copy(dt, dts, small.at[0]), pltpu.make_async_copy(rates, spd, small.at[1]),
              pltpu.make_async_copy(skip, skp, small.at[2])]
    for c in smalls:
        c.start()
    wloads = []
    for i in range(25):
        wloads.append(pltpu.make_async_copy(
            w1.at[i], wc.at[pl.ds((i // 5) * C, C), pl.ds((i % 5) * S, S)], wload.at[i]))
    w2loads = []
    for i in range(9):
        for half in range(2):
            w2loads.append(pltpu.make_async_copy(
                w2.at[i], wc2.at[pl.ds((i // 3) * C + half * S, S), pl.ds((i % 3) * C, C)],
                w2load.at[2 * i + half]))

    def send(src, dst, sems, slot_out, slot_in, where):
        return pltpu.make_async_remote_copy(
            src_ref=src, dst_ref=dst, send_sem=sems.at[0, slot_out], recv_sem=sems.at[1, slot_in],
            device_id=where, device_id_type=MESH)

    pl.semaphore_wait(barrier, len(near) + r + y)
    for p in range(ROW):
        @pl.when(p < r)
        def _(p=p):
            pl.semaphore_signal(row_ready, inc=1, device_id={"tm": base + p}, device_id_type=MESH)
    for c in range(cols):
        @pl.when(c < y)
        def _(c=c):
            pl.semaphore_signal(col_ready, inc=1, device_id={"tm": c * ROW + r}, device_id_type=MESH)
    halo_copies = [send(frames.at[:, pl.ds(14 * (1 - sy), 2)], hr.at[:, pl.ds(sy, 2)], halo, 0, 0, near[0])]
    halo_copies[0].start()
    for c in wloads:
        c.start()

    loads[0].wait()
    row_id = lax.broadcasted_iota(jnp.int32, (8 * H, 1), 0)
    slot = lax.rem(row_id, 8)
    edge = jnp.where(sx == 0, 15 - slot // 4, slot // 4)
    target = lax.rem(slot, 4) * PIX + (row_id // 8) * W + edge
    lane = lax.broadcasted_iota(jnp.int32, (8 * H, PIX), 1)
    picked = jnp.zeros((8 * H, C), F32)
    for f in range(T):
        pick = jnp.where(lane + f * PIX == target, 1.0, 0.0).astype(BF16)
        picked = picked + dot(pick, xp[f, pl.ds(2, H)].reshape(PIX, C))
    sc[...] = picked.astype(BF16).reshape(H, 8, C)

    halo_copies += [
        send(sc, hc.at[pl.ds(2, H)], halo, 1, 1, near[1]),
        send(sc.at[pl.ds(14 * (1 - sy), 2)], hc.at[pl.ds(18 * sy, 2)], halo, 2, 2, near[2]),
    ]
    for c in halo_copies[1:]:
        c.start()

    for c in smalls:
        c.wait()
    weight = jnp.broadcast_to(dts[...].reshape(1, C), (S, C))
    speed = spd[...]
    faded = None
    for f in range(T):
        v = lax.dot_general(xp[f, pl.ds(2, H)].reshape(PIX, C), weight, (((1,), (1,)), ((), ())),
                            preferred_element_type=F32)
        scaled = (jnp.maximum(v, 0.0) + jnp.log1p(jnp.exp(-jnp.abs(v)))) * speed
        decay = jnp.exp(-scaled)
        gain[f] = jnp.sqrt(one_minus_exp(2.0 * scaled))
        keep[f] = decay
        faded = decay if f == 0 else faded * decay
        fade[f] = faded
    sa[...] = faded.reshape(ROW, H, S)
    ra[r] = sa[r]

    def send_decays():
        @pl.when(r < ROW - 1)
        def _():
            pl.semaphore_wait(row_ready, ROW - 1 - r)
        for p in peers:
            send(sa.at[p], ra.at[r], sems_a, p, r, {"tm": base + p}).start()

    @pl.when(r >= ROW // 2)
    def _():
        send_decays()

    for c in wloads:
        c.wait()
    for f in range(T):
        left = jnp.concatenate([xp[f, pl.ds(dy, H)].reshape(PIX, C) for dy in range(5)], axis=1)
        fresh = gain[f] * shifted(dot(left, wc[...]), 5, S, 2)
        loc[f] = fresh if f == 0 else fresh + keep[f] * loc[f - 1]

    for c in w2loads:
        c.start()

    @pl.when(r < ROW // 2)
    def _():
        send_decays()

    for c in halo_copies:
        c.wait()
    left = jnp.concatenate([hr[:, pl.ds(k, 2)].reshape(T * 2 * W, C) for k in range(2)], axis=1)
    first = pl.multiple_of(3 * C * (1 - sy), C)
    extra = shifted(dot(left, wc[pl.ds(first, 2 * C), :]), 5, S, 2).reshape(T, 2 * W, S)
    at = pl.ds(pl.multiple_of(14 * W * (1 - sy), 2 * W), 2 * W)
    more = None
    for f in range(T):
        fresh = gain[f, at, :] * extra[f]
        more = fresh if f == 0 else fresh + keep[f, at, :] * more
        loc[f, at, :] += more
    left = jnp.concatenate([hc[pl.ds(dy, H)].reshape(8 * H, C) for dy in range(5)], axis=1)
    first = pl.multiple_of(3 * S * (1 - sx), S)
    side = dot(left, wc[:, pl.ds(first, 2 * S)]).reshape(H, 8, 2 * S)
    close = jnp.where(sx == 0, side[:, :, :S], side[:, :, S:])
    far = jnp.where(sx == 0, side[:, :, S:], side[:, :, :S])
    lane8 = lax.broadcasted_iota(jnp.int32, (1, 8, S), 1)
    outer = lane8 == 7 * (1 - sx)
    inner = lane8 == 5 * (1 - sx) + 1
    at = pl.ds(pl.multiple_of(8 * (1 - sx), 8), 8)
    gain4, keep4, loc4 = (ref.reshape(T, H, W, S) for ref in (gain, keep, loc))
    for f in range(T):
        add = jnp.where(outer, close[:, f:f + 1, :] + far[:, 4 + f:5 + f, :], 0.0)
        add = add + jnp.where(inner, far[:, f:f + 1, :], 0.0)
        fresh = gain4[f, :, at, :] * add
        more = fresh if f == 0 else fresh + keep4[f, :, at, :] * more
        loc4[f, :, at, :] += more
    sb[...] = loc[T - 1].reshape(ROW, H, S)
    for p in peers:
        send(sb.at[p], rb.at[r], sems_b, p, r, {"tm": base + p}).start()
    rb[r] = sb[r]

    for where in near:
        pl.semaphore_signal(tile_ready, inc=1, device_id=where, device_id_type=MESH)
    edge_row = pl.multiple_of(15 * W * (1 - sy), W)
    edge_x = 15 * (1 - sx)
    at_edge = lax.broadcasted_iota(jnp.int32, (1, W, S), 1) == edge_x
    ends = []
    for ref in (loc, fade):
        for f in range(T):
            ends.append(jnp.sum(jnp.where(at_edge, ref[f].reshape(H, W, S), 0.0), axis=1, keepdims=True))
    ec[...] = jnp.concatenate(ends, axis=1)
    for f in range(T):
        er[f] = loc[f, pl.ds(edge_row, W), :]
        er[T + f] = fade[f, pl.ds(edge_row, W), :]
    edge_copies = [
        send(er, ner, halo2, 0, 0, near[0]),
        send(ec, nec.at[pl.ds(1, H)], halo2, 1, 1, near[1]),
        send(ec.at[pl.ds(15 * (1 - sy), 1)], nec.at[pl.ds(17 * sy, 1)], halo2, 2, 2, near[2]),
    ]
    for c in edge_copies:
        c.start()

    for p in peers:
        send(sa.at[p], ra.at[p], sems_a, p, p, {"tm": base + p}).wait()
    total_a = ra[0]
    for k in range(1, ROW):
        total_a = total_a * ra[k]
    ta[...] = total_a
    @pl.when(y < cols - 1)
    def _():
        pl.semaphore_wait(col_ready, cols - 1 - y)
    for c in range(cols):
        @pl.when(c > y)
        def _(c=c):
            send(ta, ca.at[y], sems_ca, c, y, {"tm": c * ROW + r}).start()
    for c in w2loads:
        c.wait()

    for p in peers:
        send(sb.at[p], rb.at[p], sems_b, p, p, {"tm": base + p}).wait()
    total_b = rb[0]
    for k in range(1, ROW):
        total_b = ra[k] * total_b + rb[k]
    tb[...] = total_b
    for c in range(cols):
        @pl.when(c > y)
        def _(c=c):
            send(tb, cb.at[y], sems_cb, c, y, {"tm": c * ROW + r}).start()
    carried[...] = jnp.zeros_like(total_b)
    for c in range(cols):
        @pl.when(c < y)
        def _(c=c):
            send(ta, ca.at[c], sems_ca, c, c, {"tm": c * ROW + r}).wait_recv()
            send(tb, cb.at[c], sems_cb, c, c, {"tm": c * ROW + r}).wait_recv()
            carried[...] = ca[c] * carried[...] + cb[c]
    carry = carried[...]
    so[0] = carry
    for k in range(ROW - 1):
        carry = ra[k] * carry + rb[k]
        so[k + 1] = carry
    for p in peers:
        send(so.at[p], inc.at[r], sems_o, p, r, {"tm": base + p}).start()
    inc[r] = so[r]
    for k in range(ROW):
        se[k] = jnp.sum(jnp.where(at_edge[0], so[k], 0.0), axis=0, keepdims=True)
    pl.semaphore_wait(tile_ready, len(near))
    everyone = [r] + peers

    def to_column(p):
        return send(se.at[pl.ds(p, 1)], ie.at[pl.ds(1 + r, 1)], sems_e, p, r, {"tm": base + p, "sx": 1 - sx})

    def to_row(p):
        return send(so.at[p], ir, sems_r, p, 0, {"tm": base + p, "sy": 1 - sy})

    def to_corner(p):
        return send(se.at[pl.ds(p, 1)], ie.at[pl.ds(17 * sy, 1)], sems_c, p, 0,
                    {"tm": base + p, "sy": 1 - sy, "sx": 1 - sx})

    @pl.when(r == 15 * (1 - sy))
    def _():
        for p in everyone:
            to_row(p).start()
            to_corner(p).start()
    for p in everyone:
        to_column(p).start()
    for p in peers:
        send(so.at[p], inc.at[p], sems_o, p, p, {"tm": base + p}).wait()

    for c in range(cols):
        @pl.when(c > y)
        def _(c=c):
            send(ta, ca.at[y], sems_ca, c, y, {"tm": c * ROW + r}).wait_send()
            send(tb, cb.at[y], sems_cb, c, y, {"tm": c * ROW + r}).wait_send()

    before = inc[...].reshape(PIX, S)
    for f in range(T):
        state = loc[f] + fade[f] * before
        high = state.astype(BF16)
        low = (state - high.astype(F32)).astype(BF16)
        hid[f, pl.ds(1, H)] = jnp.concatenate([high, low], axis=1).reshape(H, W, C)

    for f in range(T):
        left = jnp.concatenate([hid[f, pl.ds(dy, H)].reshape(PIX, C) for dy in range(3)], axis=1)
        direct = skp[...] * xp[f, pl.ds(2, H)].reshape(PIX, C).astype(F32)
        acc[f] = shifted(dot(left, wc2[...]), 3, C, 1) + direct

    for c in edge_copies:
        c.wait()
    for p in everyone:
        send(se.at[pl.ds(p, 1)], ie.at[pl.ds(1 + p, 1)], sems_e, p, p, {"tm": base + p, "sx": 1 - sx}).wait()
    to_row(r).wait_recv()
    to_corner(r).wait_recv()

    @pl.when(r == 15 * (1 - sy))
    def _():
        for p in everyone:
            to_row(p).wait_send()
            to_corner(p).wait_send()
    state = ner[pl.ds(0, T)] + ner[pl.ds(T, T)] * ir[...].reshape(1, W, S)
    high = state.astype(BF16)
    hr2[...] = jnp.concatenate([high, (state - high.astype(F32)).astype(BF16)], axis=2)
    both = nec[...]
    state = both[:, :T] + both[:, T:] * ie[...]
    there = lax.broadcasted_iota(jnp.int32, (H + 2, 1, 1), 0) != 17 * sy
    state = jnp.where(there, state, 0.0)
    state = jnp.concatenate([state, jnp.zeros_like(state)], axis=1)
    high = state.astype(BF16)
    hc2[...] = jnp.concatenate([high, (state - high.astype(F32)).astype(BF16)], axis=2)
    first = pl.multiple_of(2 * C * (1 - sy), C)
    extra = shifted(dot(hr2[...].reshape(T * W, C), wc2[pl.ds(first, C), :]), 3, C, 1).reshape(T, W, C)
    at = pl.multiple_of(15 * W * (1 - sy), W)
    for f in range(T):
        acc[f, pl.ds(at, W), :] += extra[f]
    left = jnp.concatenate([hc2[pl.ds(dy, H)].reshape(8 * H, C) for dy in range(3)], axis=1)
    first = pl.multiple_of(2 * C * (1 - sx), C)
    side = dot(left, wc2[:, pl.ds(first, C)]).reshape(H, 8, C)
    at = pl.multiple_of(8 * (1 - sx), 8)
    outer = lax.broadcasted_iota(jnp.int32, (1, 8, C), 1) == 7 * (1 - sx)
    acc4 = acc.reshape(T, H, W, C)
    for f in range(T):
        acc4[f, :, pl.ds(at, 8), :] += jnp.where(outer, side[:, f:f + 1, :], 0.0)
    stores = []
    for f in range(T):
        done[f] = acc[f].reshape(H, W, C).astype(BF16)
        stores.append(pltpu.make_async_copy(done.at[f], out.at[f], store.at[f]))
        stores[f].start()
    for c in stores:
        c.wait()


def body(frames, in_kernel, dt_weight, rates, out_kernel, skip):
    cols = lax.axis_size("tm") // ROW
    hbm = pl.BlockSpec(memory_space=pltpu.HBM)

    def kernel(*refs):
        layer_kernel(cols, *refs)

    dma = pltpu.SemaphoreType.DMA
    chunk = (H, S)
    return pl.pallas_call(
        kernel,
        out_shape=jax.ShapeDtypeStruct(frames.shape, BF16),
        in_specs=[hbm] * 6,
        out_specs=hbm,
        scratch_shapes=[
            pltpu.VMEM((C,), BF16),
            pltpu.VMEM((1, S), F32),
            pltpu.VMEM((1, C), F32),
            pltpu.VMEM(chunk, F32),
            pltpu.VMEM((T, H + 4, W, C), BF16),
            pltpu.VMEM((5 * C, 5 * S), BF16),
            pltpu.VMEM((3 * C, 3 * C), BF16),
            pltpu.VMEM((T, 3, W, C), BF16),
            pltpu.VMEM((H + 4, 8, C), BF16),
            pltpu.VMEM((H, 8, C), BF16),
            pltpu.VMEM((T, PIX, S), F32),
            pltpu.VMEM((T, PIX, S), F32),
            pltpu.VMEM((T, PIX, S), F32),
            pltpu.VMEM((T, PIX, S), F32),
            pltpu.VMEM((T, H + 2, W, C), BF16),
            pltpu.VMEM((T, W, C), BF16),
            pltpu.VMEM((H + 2, 8, C), BF16),
            pltpu.VMEM((T, PIX, C), F32),
            pltpu.VMEM((T, H, W, C), BF16),
            pltpu.VMEM((2 * T, W, S), F32),
            pltpu.VMEM((H, 2 * T, S), F32),
            pltpu.VMEM((2 * T, W, S), F32),
            pltpu.VMEM((H + 2, 2 * T, S), F32),
            pltpu.VMEM((ROW, 1, S), F32),
            pltpu.VMEM((H + 2, 1, S), F32),
            pltpu.VMEM(chunk, F32),
            pltpu.VMEM((ROW,) + chunk, F32),
            pltpu.VMEM((ROW,) + chunk, F32),
            pltpu.VMEM((ROW,) + chunk, F32),
            pltpu.VMEM((ROW,) + chunk, F32),
            pltpu.VMEM((cols,) + chunk, F32),
            pltpu.VMEM((cols,) + chunk, F32),
            pltpu.VMEM(chunk, F32),
            pltpu.VMEM(chunk, F32),
            pltpu.VMEM((ROW,) + chunk, F32),
            pltpu.VMEM((ROW,) + chunk, F32),
            pltpu.SemaphoreType.REGULAR,
            pltpu.SemaphoreType.REGULAR,
            pltpu.SemaphoreType.REGULAR,
            dma((3,)),
            dma((T,)),
            dma,
            dma((25,)),
            dma((18,)),
            dma((2, 3)),
            dma((2, 3)),
            dma((2, ROW)),
            dma((2, ROW)),
            dma((2, cols)),
            dma((2, cols)),
            dma((2, ROW)),
            dma((2, ROW)),
            dma((2, ROW)),
            dma((2, ROW)),
        ],
        compiler_params=pltpu.CompilerParams(
            collective_id=0, has_side_effects=True, vmem_limit_bytes=67_000_000),
    )(frames, in_kernel.reshape(25, C, S), dt_weight, rates.reshape(1, S),
      out_kernel.reshape(9, S, C), skip.reshape(1, C))


def solution(mesh):
    return jax.shard_map(
        body,
        mesh=mesh,
        in_specs=(P("tm", "sy", "sx", None), P(), P(), P(), P(), P()),
        out_specs=P("tm", "sy", "sx", None),
        check_vma=False,
    )
```

```python
import jax
import jax.numpy as jnp
from jax import lax
from jax.experimental import pallas as pl
from jax.experimental.pallas import tpu as pltpu
from jax.sharding import PartitionSpec as P

ROW = 16
T, H, W = 4, 16, 16
PIX = H * W
C, S = 256, 128
MESH = pl.DeviceIdType.MESH
ORDER = [8, 7, 9, 6, 10, 5, 11, 4, 12, 3, 13, 2, 14, 1, 15]
F32 = jnp.float32
BF16 = jnp.bfloat16


def dot(a, b):
    return jnp.dot(a, b, preferred_element_type=F32)


def shifted(wide, taps, width, reach):
    rows = wide.shape[0]
    column = lax.rem(lax.broadcasted_iota(jnp.int32, (rows, width), 0), W)
    total = wide[:, reach * width:(reach + 1) * width]
    for tap in range(taps):
        move = tap - reach
        if move == 0:
            continue
        part = pltpu.roll(wide[:, tap * width:(tap + 1) * width], (-move) % rows, 0)
        inside = (column + move >= 0) & (column + move < W)
        total = total + jnp.where(inside, part, 0.0)
    return total


def one_minus_exp(u):
    series = u * (1.0 - u * (1 / 2) * (1.0 - u * (1 / 3) * (1.0 - u * (1 / 4) * (1.0 - u * (1 / 5) * (
        1.0 - u * (1 / 6) * (1.0 - u * (1 / 7) * (1.0 - u * (1 / 8))))))))
    return jnp.where(u < 0.5, series, 1.0 - jnp.exp(-u))


def layer_kernel(cols, frames, w1, dt, rates, w2, skip, out,
                 dts, spd, skp, carried, xp, wc, wc2, hr, hc, sc, gain, fade, keep, loc, hid, hr2, hc2, acc, done, er, ec, ner, nec, se, ie, ir,
                 sa, sb, ra, rb, ca, cb, ta, tb, so, inc,
                 row_ready, col_ready, tile_ready, small, store, load, wload, w2load, halo, halo2, sems_a, sems_b, sems_ca, sems_cb, sems_o, sems_e, sems_r, sems_c):
    me = lax.axis_index("tm")
    sy = lax.axis_index("sy")
    sx = lax.axis_index("sx")
    r = lax.rem(me, ROW)
    y = lax.div(me, ROW)
    base = me - r
    peers = [lax.rem(r + d, ROW) for d in ORDER]
    near = [{"sy": 1 - sy}, {"sx": 1 - sx}, {"sy": 1 - sy, "sx": 1 - sx}]

    zrow = jnp.zeros((W, C), BF16)
    for f in range(T):
        for row in (0, 1, 18, 19):
            xp[f, row] = zrow
        hr[f, 2 * sy] = zrow
        hid[f, 0] = zrow
        hid[f, 17] = zrow
    for row in range(2):
        hc[18 * sy + row] = zrow[:8]
    nec[17 * sy] = jnp.zeros((8, S), F32)
    ie[17 * sy] = jnp.zeros((1, S), F32)

    barrier = pltpu.get_barrier_semaphore()
    for where in near:
        pl.semaphore_signal(barrier, inc=1, device_id=where, device_id_type=MESH)
    for p in range(ROW):
        @pl.when(p > r)
        def _(p=p):
            pl.semaphore_signal(barrier, inc=1, device_id={"tm": base + p}, device_id_type=MESH)
    for c in range(cols):
        @pl.when(c > y)
        def _(c=c):
            pl.semaphore_signal(barrier, inc=1, device_id={"tm": c * ROW + r}, device_id_type=MESH)

    loads = [pltpu.make_async_copy(frames, xp.at[:, pl.ds(2, H)], load)]
    loads[0].start()
    smalls = [pltpu.make_async_copy(dt, dts, small.at[0]), pltpu.make_async_copy(rates, spd, small.at[1]),
              pltpu.make_async_copy(skip, skp, small.at[2])]
    for c in smalls:
        c.start()
    wloads = []
    for i in range(25):
        wloads.append(pltpu.make_async_copy(
            w1.at[i], wc.at[pl.ds((i // 5) * C, C), pl.ds((i % 5) * S, S)], wload.at[i]))
    w2loads = []
    for i in range(9):
        for half in range(2):
            w2loads.append(pltpu.make_async_copy(
                w2.at[i], wc2.at[pl.ds((i // 3) * C + half * S, S), pl.ds((i % 3) * C, C)],
                w2load.at[2 * i + half]))

    def send(src, dst, sems, slot_out, slot_in, where):
        return pltpu.make_async_remote_copy(
            src_ref=src, dst_ref=dst, send_sem=sems.at[0, slot_out], recv_sem=sems.at[1, slot_in],
            device_id=where, device_id_type=MESH)

    pl.semaphore_wait(barrier, len(near) + r + y)
    for p in range(ROW):
        @pl.when(p < r)
        def _(p=p):
            pl.semaphore_signal(row_ready, inc=1, device_id={"tm": base + p}, device_id_type=MESH)
    for c in range(cols):
        @pl.when(c < y)
        def _(c=c):
            pl.semaphore_signal(col_ready, inc=1, device_id={"tm": c * ROW + r}, device_id_type=MESH)
    halo_copies = [send(frames.at[:, pl.ds(14 * (1 - sy), 2)], hr.at[:, pl.ds(sy, 2)], halo, 0, 0, near[0])]
    halo_copies[0].start()
    for c in wloads:
        c.start()

    loads[0].wait()
    row_id = lax.broadcasted_iota(jnp.int32, (8 * H, 1), 0)
    slot = lax.rem(row_id, 8)
    edge = jnp.where(sx == 0, 15 - slot // 4, slot // 4)
    target = lax.rem(slot, 4) * PIX + (row_id // 8) * W + edge
    lane = lax.broadcasted_iota(jnp.int32, (8 * H, PIX), 1)
    picked = jnp.zeros((8 * H, C), F32)
    for f in range(T):
        pick = jnp.where(lane + f * PIX == target, 1.0, 0.0).astype(BF16)
        picked = picked + dot(pick, xp[f, pl.ds(2, H)].reshape(PIX, C))
    sc[...] = picked.astype(BF16).reshape(H, 8, C)

    halo_copies += [
        send(sc, hc.at[pl.ds(2, H)], halo, 1, 1, near[1]),
        send(sc.at[pl.ds(14 * (1 - sy), 2)], hc.at[pl.ds(18 * sy, 2)], halo, 2, 2, near[2]),
    ]
    for c in halo_copies[1:]:
        c.start()

    for c in smalls:
        c.wait()
    weight = jnp.broadcast_to(dts[...].reshape(1, C), (S, C))
    speed = spd[...]
    faded = None
    for f in range(T):
        v = lax.dot_general(xp[f, pl.ds(2, H)].reshape(PIX, C), weight, (((1,), (1,)), ((), ())),
                            preferred_element_type=F32)
        scaled = (jnp.maximum(v, 0.0) + jnp.log1p(jnp.exp(-jnp.abs(v)))) * speed
        decay = jnp.exp(-scaled)
        gain[f] = jnp.sqrt(one_minus_exp(2.0 * scaled))
        keep[f] = decay
        faded = decay if f == 0 else faded * decay
        fade[f] = faded
    sa[...] = faded.reshape(ROW, H, S)
    ra[r] = sa[r]

    def send_decays():
        @pl.when(r < ROW - 1)
        def _():
            pl.semaphore_wait(row_ready, ROW - 1 - r)
        for p in peers:
            send(sa.at[p], ra.at[r], sems_a, p, r, {"tm": base + p}).start()

    @pl.when(r >= ROW // 2)
    def _():
        send_decays()

    for c in wloads:
        c.wait()
    for f in range(T):
        left = jnp.concatenate([xp[f, pl.ds(dy, H)].reshape(PIX, C) for dy in range(5)], axis=1)
        fresh = gain[f] * shifted(dot(left, wc[...]), 5, S, 2)
        loc[f] = fresh if f == 0 else fresh + keep[f] * loc[f - 1]

    for c in w2loads:
        c.start()

    @pl.when(r < ROW // 2)
    def _():
        send_decays()

    for c in halo_copies:
        c.wait()
    left = jnp.concatenate([hr[:, pl.ds(k, 2)].reshape(T * 2 * W, C) for k in range(2)], axis=1)
    first = pl.multiple_of(3 * C * (1 - sy), C)
    extra = shifted(dot(left, wc[pl.ds(first, 2 * C), :]), 5, S, 2).reshape(T, 2 * W, S)
    at = pl.ds(pl.multiple_of(14 * W * (1 - sy), 2 * W), 2 * W)
    more = None
    for f in range(T):
        fresh = gain[f, at, :] * extra[f]
        more = fresh if f == 0 else fresh + keep[f, at, :] * more
        loc[f, at, :] += more
    left = jnp.concatenate([hc[pl.ds(dy, H)].reshape(8 * H, C) for dy in range(5)], axis=1)
    first = pl.multiple_of(3 * S * (1 - sx), S)
    side = dot(left, wc[:, pl.ds(first, 2 * S)]).reshape(H, 8, 2 * S)
    close = jnp.where(sx == 0, side[:, :, :S], side[:, :, S:])
    far = jnp.where(sx == 0, side[:, :, S:], side[:, :, :S])
    lane8 = lax.broadcasted_iota(jnp.int32, (1, 8, S), 1)
    outer = lane8 == 7 * (1 - sx)
    inner = lane8 == 5 * (1 - sx) + 1
    at = pl.ds(pl.multiple_of(8 * (1 - sx), 8), 8)
    gain4, keep4, loc4 = (ref.reshape(T, H, W, S) for ref in (gain, keep, loc))
    for f in range(T):
        add = jnp.where(outer, close[:, f:f + 1, :] + far[:, 4 + f:5 + f, :], 0.0)
        add = add + jnp.where(inner, far[:, f:f + 1, :], 0.0)
        fresh = gain4[f, :, at, :] * add
        more = fresh if f == 0 else fresh + keep4[f, :, at, :] * more
        loc4[f, :, at, :] += more
    sb[...] = loc[T - 1].reshape(ROW, H, S)
    for p in peers:
        send(sb.at[p], rb.at[r], sems_b, p, r, {"tm": base + p}).start()
    rb[r] = sb[r]

    for where in near:
        pl.semaphore_signal(tile_ready, inc=1, device_id=where, device_id_type=MESH)
    edge_row = pl.multiple_of(15 * W * (1 - sy), W)
    edge_x = 15 * (1 - sx)
    at_edge = lax.broadcasted_iota(jnp.int32, (1, W, S), 1) == edge_x
    ends = []
    for ref in (loc, fade):
        for f in range(T):
            ends.append(jnp.sum(jnp.where(at_edge, ref[f].reshape(H, W, S), 0.0), axis=1, keepdims=True))
    ec[...] = jnp.concatenate(ends, axis=1)
    for f in range(T):
        er[f] = loc[f, pl.ds(edge_row, W), :]
        er[T + f] = fade[f, pl.ds(edge_row, W), :]
    edge_copies = [
        send(er, ner, halo2, 0, 0, near[0]),
        send(ec, nec.at[pl.ds(1, H)], halo2, 1, 1, near[1]),
        send(ec.at[pl.ds(15 * (1 - sy), 1)], nec.at[pl.ds(17 * sy, 1)], halo2, 2, 2, near[2]),
    ]
    for c in edge_copies:
        c.start()

    for p in peers:
        send(sa.at[p], ra.at[p], sems_a, p, p, {"tm": base + p}).wait()
    total_a = ra[0]
    for k in range(1, ROW):
        total_a = total_a * ra[k]
    ta[...] = total_a
    @pl.when(y < cols - 1)
    def _():
        pl.semaphore_wait(col_ready, cols - 1 - y)
    for c in range(cols):
        @pl.when(c > y)
        def _(c=c):
            send(ta, ca.at[y], sems_ca, c, y, {"tm": c * ROW + r}).start()
    for c in w2loads:
        c.wait()

    for p in peers:
        send(sb.at[p], rb.at[p], sems_b, p, p, {"tm": base + p}).wait()
    total_b = rb[0]
    for k in range(1, ROW):
        total_b = ra[k] * total_b + rb[k]
    tb[...] = total_b
    for c in range(cols):
        @pl.when(c > y)
        def _(c=c):
            send(tb, cb.at[y], sems_cb, c, y, {"tm": c * ROW + r}).start()
    carried[...] = jnp.zeros_like(total_b)
    for c in range(cols):
        @pl.when(c < y)
        def _(c=c):
            send(ta, ca.at[c], sems_ca, c, c, {"tm": c * ROW + r}).wait_recv()
            send(tb, cb.at[c], sems_cb, c, c, {"tm": c * ROW + r}).wait_recv()
            carried[...] = ca[c] * carried[...] + cb[c]
    carry = carried[...]
    so[0] = carry
    for k in range(ROW - 1):
        carry = ra[k] * carry + rb[k]
        so[k + 1] = carry
    for p in range(ROW):
        @pl.when(p != r)
        def _(p=p):
            send(so.at[p], inc.at[r], sems_o, p, r, {"tm": base + p}).start()
    inc[r] = so[r]
    for k in range(ROW):
        se[k] = jnp.sum(jnp.where(at_edge[0], so[k], 0.0), axis=0, keepdims=True)
    pl.semaphore_wait(tile_ready, len(near))
    everyone = list(range(ROW))

    def to_column(p):
        return send(se.at[pl.ds(p, 1)], ie.at[pl.ds(1 + r, 1)], sems_e, p, r, {"tm": base + p, "sx": 1 - sx})

    def to_row(p):
        return send(so.at[p], ir, sems_r, p, 0, {"tm": base + p, "sy": 1 - sy})

    def to_corner(p):
        return send(se.at[pl.ds(p, 1)], ie.at[pl.ds(17 * sy, 1)], sems_c, p, 0,
                    {"tm": base + p, "sy": 1 - sy, "sx": 1 - sx})

    @pl.when(r == 15 * (1 - sy))
    def _():
        for p in everyone:
            to_row(p).start()
            to_corner(p).start()
    for p in everyone:
        to_column(p).start()
    for p in peers:
        send(so.at[p], inc.at[p], sems_o, p, p, {"tm": base + p}).wait()

    for c in range(cols):
        @pl.when(c > y)
        def _(c=c):
            send(ta, ca.at[y], sems_ca, c, y, {"tm": c * ROW + r}).wait_send()
            send(tb, cb.at[y], sems_cb, c, y, {"tm": c * ROW + r}).wait_send()

    before = inc[...].reshape(PIX, S)
    for f in range(T):
        state = loc[f] + fade[f] * before
        high = state.astype(BF16)
        low = (state - high.astype(F32)).astype(BF16)
        hid[f, pl.ds(1, H)] = jnp.concatenate([high, low], axis=1).reshape(H, W, C)

    for f in range(T):
        left = jnp.concatenate([hid[f, pl.ds(dy, H)].reshape(PIX, C) for dy in range(3)], axis=1)
        direct = skp[...] * xp[f, pl.ds(2, H)].reshape(PIX, C).astype(F32)
        acc[f] = shifted(dot(left, wc2[...]), 3, C, 1) + direct

    for c in edge_copies:
        c.wait()
    for p in everyone:
        send(se.at[pl.ds(p, 1)], ie.at[pl.ds(1 + p, 1)], sems_e, p, p, {"tm": base + p, "sx": 1 - sx}).wait()
    to_row(r).wait_recv()
    to_corner(r).wait_recv()

    @pl.when(r == 15 * (1 - sy))
    def _():
        for p in everyone:
            to_row(p).wait_send()
            to_corner(p).wait_send()
    state = ner[pl.ds(0, T)] + ner[pl.ds(T, T)] * ir[...].reshape(1, W, S)
    high = state.astype(BF16)
    hr2[...] = jnp.concatenate([high, (state - high.astype(F32)).astype(BF16)], axis=2)
    both = nec[...]
    state = both[:, :T] + both[:, T:] * ie[...]
    there = lax.broadcasted_iota(jnp.int32, (H + 2, 1, 1), 0) != 17 * sy
    state = jnp.where(there, state, 0.0)
    state = jnp.concatenate([state, jnp.zeros_like(state)], axis=1)
    high = state.astype(BF16)
    hc2[...] = jnp.concatenate([high, (state - high.astype(F32)).astype(BF16)], axis=2)
    first = pl.multiple_of(2 * C * (1 - sy), C)
    extra = shifted(dot(hr2[...].reshape(T * W, C), wc2[pl.ds(first, C), :]), 3, C, 1).reshape(T, W, C)
    at = pl.multiple_of(15 * W * (1 - sy), W)
    for f in range(T):
        acc[f, pl.ds(at, W), :] += extra[f]
    left = jnp.concatenate([hc2[pl.ds(dy, H)].reshape(8 * H, C) for dy in range(3)], axis=1)
    first = pl.multiple_of(2 * C * (1 - sx), C)
    side = dot(left, wc2[:, pl.ds(first, C)]).reshape(H, 8, C)
    at = pl.multiple_of(8 * (1 - sx), 8)
    outer = lax.broadcasted_iota(jnp.int32, (1, 8, C), 1) == 7 * (1 - sx)
    acc4 = acc.reshape(T, H, W, C)
    for f in range(T):
        acc4[f, :, pl.ds(at, 8), :] += jnp.where(outer, side[:, f:f + 1, :], 0.0)
    stores = []
    for f in range(T):
        done[f] = acc[f].reshape(H, W, C).astype(BF16)
        stores.append(pltpu.make_async_copy(done.at[f], out.at[f], store.at[f]))
        stores[f].start()
    for c in stores:
        c.wait()


def body(frames, in_kernel, dt_weight, rates, out_kernel, skip):
    cols = lax.axis_size("tm") // ROW
    hbm = pl.BlockSpec(memory_space=pltpu.HBM)

    def kernel(*refs):
        layer_kernel(cols, *refs)

    dma = pltpu.SemaphoreType.DMA
    chunk = (H, S)
    return pl.pallas_call(
        kernel,
        out_shape=jax.ShapeDtypeStruct(frames.shape, BF16),
        in_specs=[hbm] * 6,
        out_specs=hbm,
        scratch_shapes=[
            pltpu.VMEM((C,), BF16),
            pltpu.VMEM((1, S), F32),
            pltpu.VMEM((1, C), F32),
            pltpu.VMEM(chunk, F32),
            pltpu.VMEM((T, H + 4, W, C), BF16),
            pltpu.VMEM((5 * C, 5 * S), BF16),
            pltpu.VMEM((3 * C, 3 * C), BF16),
            pltpu.VMEM((T, 3, W, C), BF16),
            pltpu.VMEM((H + 4, 8, C), BF16),
            pltpu.VMEM((H, 8, C), BF16),
            pltpu.VMEM((T, PIX, S), F32),
            pltpu.VMEM((T, PIX, S), F32),
            pltpu.VMEM((T, PIX, S), F32),
            pltpu.VMEM((T, PIX, S), F32),
            pltpu.VMEM((T, H + 2, W, C), BF16),
            pltpu.VMEM((T, W, C), BF16),
            pltpu.VMEM((H + 2, 8, C), BF16),
            pltpu.VMEM((T, PIX, C), F32),
            pltpu.VMEM((T, H, W, C), BF16),
            pltpu.VMEM((2 * T, W, S), F32),
            pltpu.VMEM((H, 2 * T, S), F32),
            pltpu.VMEM((2 * T, W, S), F32),
            pltpu.VMEM((H + 2, 2 * T, S), F32),
            pltpu.VMEM((ROW, 1, S), F32),
            pltpu.VMEM((H + 2, 1, S), F32),
            pltpu.VMEM(chunk, F32),
            pltpu.VMEM((ROW,) + chunk, F32),
            pltpu.VMEM((ROW,) + chunk, F32),
            pltpu.VMEM((ROW,) + chunk, F32),
            pltpu.VMEM((ROW,) + chunk, F32),
            pltpu.VMEM((cols,) + chunk, F32),
            pltpu.VMEM((cols,) + chunk, F32),
            pltpu.VMEM(chunk, F32),
            pltpu.VMEM(chunk, F32),
            pltpu.VMEM((ROW,) + chunk, F32),
            pltpu.VMEM((ROW,) + chunk, F32),
            pltpu.SemaphoreType.REGULAR,
            pltpu.SemaphoreType.REGULAR,
            pltpu.SemaphoreType.REGULAR,
            dma((3,)),
            dma((T,)),
            dma,
            dma((25,)),
            dma((18,)),
            dma((2, 3)),
            dma((2, 3)),
            dma((2, ROW)),
            dma((2, ROW)),
            dma((2, cols)),
            dma((2, cols)),
            dma((2, ROW)),
            dma((2, ROW)),
            dma((2, ROW)),
            dma((2, ROW)),
        ],
        compiler_params=pltpu.CompilerParams(
            collective_id=0, has_side_effects=True, vmem_limit_bytes=67_000_000),
    )(frames, in_kernel.reshape(25, C, S), dt_weight, rates.reshape(1, S),
      out_kernel.reshape(9, S, C), skip.reshape(1, C))


def solution(mesh):
    return jax.shard_map(
        body,
        mesh=mesh,
        in_specs=(P("tm", "sy", "sx", None), P(), P(), P(), P(), P()),
        out_specs=P("tm", "sy", "sx", None),
        check_vma=False,
    )
```

```python
import jax
import jax.numpy as jnp
from jax import lax
from jax.experimental import pallas as pl
from jax.experimental.pallas import tpu as pltpu
from jax.sharding import PartitionSpec as P

ROW = 16
T, H, W = 4, 16, 16
PIX = H * W
C, S = 256, 128
MESH = pl.DeviceIdType.MESH
ORDER = [8, 9, 7, 4, 12, 6, 10, 5, 11, 2, 14, 3, 13, 1, 15]
F32 = jnp.float32
BF16 = jnp.bfloat16


def dot(a, b):
    return jnp.dot(a, b, preferred_element_type=F32)


def shifted(wide, taps, width, reach):
    rows = wide.shape[0]
    column = lax.rem(lax.broadcasted_iota(jnp.int32, (rows, width), 0), W)
    total = wide[:, reach * width:(reach + 1) * width]
    for tap in range(taps):
        move = tap - reach
        if move == 0:
            continue
        part = pltpu.roll(wide[:, tap * width:(tap + 1) * width], (-move) % rows, 0)
        inside = (column + move >= 0) & (column + move < W)
        total = total + jnp.where(inside, part, 0.0)
    return total


def one_minus_exp(u):
    series = u * (1.0 - u * (1 / 2) * (1.0 - u * (1 / 3) * (1.0 - u * (1 / 4) * (1.0 - u * (1 / 5) * (
        1.0 - u * (1 / 6) * (1.0 - u * (1 / 7) * (1.0 - u * (1 / 8))))))))
    return jnp.where(u < 0.5, series, 1.0 - jnp.exp(-u))


def layer_kernel(cols, frames, w1, dt, rates, w2, skip, out,
                 dts, spd, skp, carried, xp, wc, wc2, hr, hc, sc, gain, fade, keep, loc, hid, hr2, hc2, acc, done, er, ec, ner, nec, se, ie, ir,
                 sa, sb, ra, rb, ca, cb, ta, tb, so, inc,
                 row_ready, col_ready, tile_ready, small, store, load, wload, w2load, halo, halo2, sems_a, sems_b, sems_ca, sems_cb, sems_o, sems_e, sems_r, sems_c):
    me = lax.axis_index("tm")
    sy = lax.axis_index("sy")
    sx = lax.axis_index("sx")
    r = lax.rem(me, ROW)
    y = lax.div(me, ROW)
    base = me - r
    peers = [lax.rem(r + d, ROW) for d in ORDER]
    near = [{"sy": 1 - sy}, {"sx": 1 - sx}, {"sy": 1 - sy, "sx": 1 - sx}]

    zrow = jnp.zeros((W, C), BF16)
    for f in range(T):
        for row in (0, 1, 18, 19):
            xp[f, row] = zrow
        hr[f, 2 * sy] = zrow
        hid[f, 0] = zrow
        hid[f, 17] = zrow
    for row in range(2):
        hc[18 * sy + row] = zrow[:8]
    nec[17 * sy] = jnp.zeros((8, S), F32)
    ie[17 * sy] = jnp.zeros((1, S), F32)

    barrier = pltpu.get_barrier_semaphore()
    for where in near:
        pl.semaphore_signal(barrier, inc=1, device_id=where, device_id_type=MESH)
    for p in range(ROW):
        @pl.when(p > r)
        def _(p=p):
            pl.semaphore_signal(barrier, inc=1, device_id={"tm": base + p}, device_id_type=MESH)
    for c in range(cols):
        @pl.when(c > y)
        def _(c=c):
            pl.semaphore_signal(barrier, inc=1, device_id={"tm": c * ROW + r}, device_id_type=MESH)

    loads = [pltpu.make_async_copy(frames, xp.at[:, pl.ds(2, H)], load)]
    loads[0].start()
    smalls = [pltpu.make_async_copy(dt, dts, small.at[0]), pltpu.make_async_copy(rates, spd, small.at[1]),
              pltpu.make_async_copy(skip, skp, small.at[2])]
    for c in smalls:
        c.start()
    wloads = []
    for i in range(25):
        wloads.append(pltpu.make_async_copy(
            w1.at[i], wc.at[pl.ds((i // 5) * C, C), pl.ds((i % 5) * S, S)], wload.at[i]))
    w2loads = []
    for i in range(9):
        for half in range(2):
            w2loads.append(pltpu.make_async_copy(
                w2.at[i], wc2.at[pl.ds((i // 3) * C + half * S, S), pl.ds((i % 3) * C, C)],
                w2load.at[2 * i + half]))

    def send(src, dst, sems, slot_out, slot_in, where):
        return pltpu.make_async_remote_copy(
            src_ref=src, dst_ref=dst, send_sem=sems.at[0, slot_out], recv_sem=sems.at[1, slot_in],
            device_id=where, device_id_type=MESH)

    pl.semaphore_wait(barrier, len(near) + r + y)
    for p in range(ROW):
        @pl.when(p < r)
        def _(p=p):
            pl.semaphore_signal(row_ready, inc=1, device_id={"tm": base + p}, device_id_type=MESH)
    for c in range(cols):
        @pl.when(c < y)
        def _(c=c):
            pl.semaphore_signal(col_ready, inc=1, device_id={"tm": c * ROW + r}, device_id_type=MESH)
    halo_copies = [send(frames.at[:, pl.ds(14 * (1 - sy), 2)], hr.at[:, pl.ds(sy, 2)], halo, 0, 0, near[0])]
    halo_copies[0].start()
    for c in wloads:
        c.start()

    loads[0].wait()
    row_id = lax.broadcasted_iota(jnp.int32, (8 * H, 1), 0)
    slot = lax.rem(row_id, 8)
    edge = jnp.where(sx == 0, 15 - slot // 4, slot // 4)
    target = lax.rem(slot, 4) * PIX + (row_id // 8) * W + edge
    lane = lax.broadcasted_iota(jnp.int32, (8 * H, PIX), 1)
    picked = jnp.zeros((8 * H, C), F32)
    for f in range(T):
        pick = jnp.where(lane + f * PIX == target, 1.0, 0.0).astype(BF16)
        picked = picked + dot(pick, xp[f, pl.ds(2, H)].reshape(PIX, C))
    sc[...] = picked.astype(BF16).reshape(H, 8, C)

    halo_copies += [
        send(sc, hc.at[pl.ds(2, H)], halo, 1, 1, near[1]),
        send(sc.at[pl.ds(14 * (1 - sy), 2)], hc.at[pl.ds(18 * sy, 2)], halo, 2, 2, near[2]),
    ]
    for c in halo_copies[1:]:
        c.start()

    for c in smalls:
        c.wait()
    weight = jnp.broadcast_to(dts[...].reshape(1, C), (S, C))
    speed = spd[...]
    faded = None
    for f in range(T):
        v = lax.dot_general(xp[f, pl.ds(2, H)].reshape(PIX, C), weight, (((1,), (1,)), ((), ())),
                            preferred_element_type=F32)
        scaled = (jnp.maximum(v, 0.0) + jnp.log1p(jnp.exp(-jnp.abs(v)))) * speed
        decay = jnp.exp(-scaled)
        gain[f] = jnp.sqrt(one_minus_exp(2.0 * scaled))
        keep[f] = decay
        faded = decay if f == 0 else faded * decay
        fade[f] = faded
    sa[...] = faded.reshape(ROW, H, S)
    ra[r] = sa[r]

    def send_decays():
        @pl.when(r < ROW - 1)
        def _():
            pl.semaphore_wait(row_ready, ROW - 1 - r)
        for p in peers:
            send(sa.at[p], ra.at[r], sems_a, p, r, {"tm": base + p}).start()

    @pl.when(r >= ROW // 2)
    def _():
        send_decays()

    for c in wloads:
        c.wait()
    for f in range(T):
        left = jnp.concatenate([xp[f, pl.ds(dy, H)].reshape(PIX, C) for dy in range(5)], axis=1)
        fresh = gain[f] * shifted(dot(left, wc[...]), 5, S, 2)
        loc[f] = fresh if f == 0 else fresh + keep[f] * loc[f - 1]

    for c in w2loads:
        c.start()

    @pl.when(r < ROW // 2)
    def _():
        send_decays()

    for c in halo_copies:
        c.wait()
    left = jnp.concatenate([hr[:, pl.ds(k, 2)].reshape(T * 2 * W, C) for k in range(2)], axis=1)
    first = pl.multiple_of(3 * C * (1 - sy), C)
    extra = shifted(dot(left, wc[pl.ds(first, 2 * C), :]), 5, S, 2).reshape(T, 2 * W, S)
    at = pl.ds(pl.multiple_of(14 * W * (1 - sy), 2 * W), 2 * W)
    more = None
    for f in range(T):
        fresh = gain[f, at, :] * extra[f]
        more = fresh if f == 0 else fresh + keep[f, at, :] * more
        loc[f, at, :] += more
    left = jnp.concatenate([hc[pl.ds(dy, H)].reshape(8 * H, C) for dy in range(5)], axis=1)
    first = pl.multiple_of(3 * S * (1 - sx), S)
    side = dot(left, wc[:, pl.ds(first, 2 * S)]).reshape(H, 8, 2 * S)
    close = jnp.where(sx == 0, side[:, :, :S], side[:, :, S:])
    far = jnp.where(sx == 0, side[:, :, S:], side[:, :, :S])
    lane8 = lax.broadcasted_iota(jnp.int32, (1, 8, S), 1)
    outer = lane8 == 7 * (1 - sx)
    inner = lane8 == 5 * (1 - sx) + 1
    at = pl.ds(pl.multiple_of(8 * (1 - sx), 8), 8)
    gain4, keep4, loc4 = (ref.reshape(T, H, W, S) for ref in (gain, keep, loc))
    for f in range(T):
        add = jnp.where(outer, close[:, f:f + 1, :] + far[:, 4 + f:5 + f, :], 0.0)
        add = add + jnp.where(inner, far[:, f:f + 1, :], 0.0)
        fresh = gain4[f, :, at, :] * add
        more = fresh if f == 0 else fresh + keep4[f, :, at, :] * more
        loc4[f, :, at, :] += more
    sb[...] = loc[T - 1].reshape(ROW, H, S)
    for p in peers:
        send(sb.at[p], rb.at[r], sems_b, p, r, {"tm": base + p}).start()
    rb[r] = sb[r]

    for where in near:
        pl.semaphore_signal(tile_ready, inc=1, device_id=where, device_id_type=MESH)
    edge_row = pl.multiple_of(15 * W * (1 - sy), W)
    edge_x = 15 * (1 - sx)
    at_edge = lax.broadcasted_iota(jnp.int32, (1, W, S), 1) == edge_x
    ends = []
    for ref in (loc, fade):
        for f in range(T):
            ends.append(jnp.sum(jnp.where(at_edge, ref[f].reshape(H, W, S), 0.0), axis=1, keepdims=True))
    ec[...] = jnp.concatenate(ends, axis=1)
    for f in range(T):
        er[f] = loc[f, pl.ds(edge_row, W), :]
        er[T + f] = fade[f, pl.ds(edge_row, W), :]
    edge_copies = [
        send(er, ner, halo2, 0, 0, near[0]),
        send(ec, nec.at[pl.ds(1, H)], halo2, 1, 1, near[1]),
        send(ec.at[pl.ds(15 * (1 - sy), 1)], nec.at[pl.ds(17 * sy, 1)], halo2, 2, 2, near[2]),
    ]
    for c in edge_copies:
        c.start()

    for p in peers:
        send(sa.at[p], ra.at[p], sems_a, p, p, {"tm": base + p}).wait()
    total_a = ra[0]
    for k in range(1, ROW):
        total_a = total_a * ra[k]
    ta[...] = total_a
    @pl.when(y < cols - 1)
    def _():
        pl.semaphore_wait(col_ready, cols - 1 - y)
    for c in range(cols):
        @pl.when(c > y)
        def _(c=c):
            send(ta, ca.at[y], sems_ca, c, y, {"tm": c * ROW + r}).start()
    for c in w2loads:
        c.wait()

    for p in peers:
        send(sb.at[p], rb.at[p], sems_b, p, p, {"tm": base + p}).wait()
    total_b = rb[0]
    for k in range(1, ROW):
        total_b = ra[k] * total_b + rb[k]
    tb[...] = total_b
    for c in range(cols):
        @pl.when(c > y)
        def _(c=c):
            send(tb, cb.at[y], sems_cb, c, y, {"tm": c * ROW + r}).start()
    carried[...] = jnp.zeros_like(total_b)
    for c in range(cols):
        @pl.when(c < y)
        def _(c=c):
            send(ta, ca.at[c], sems_ca, c, c, {"tm": c * ROW + r}).wait_recv()
            send(tb, cb.at[c], sems_cb, c, c, {"tm": c * ROW + r}).wait_recv()
            carried[...] = ca[c] * carried[...] + cb[c]
    carry = carried[...]
    so[0] = carry
    for k in range(ROW - 1):
        carry = ra[k] * carry + rb[k]
        so[k + 1] = carry
    for p in range(ROW):
        @pl.when(p != r)
        def _(p=p):
            send(so.at[p], inc.at[r], sems_o, p, r, {"tm": base + p}).start()
    inc[r] = so[r]
    for k in range(ROW):
        se[k] = jnp.sum(jnp.where(at_edge[0], so[k], 0.0), axis=0, keepdims=True)
    pl.semaphore_wait(tile_ready, len(near))
    everyone = list(range(ROW))

    def to_column(p):
        return send(se.at[pl.ds(p, 1)], ie.at[pl.ds(1 + r, 1)], sems_e, p, r, {"tm": base + p, "sx": 1 - sx})

    def to_row(p):
        return send(so.at[p], ir, sems_r, p, 0, {"tm": base + p, "sy": 1 - sy})

    def to_corner(p):
        return send(se.at[pl.ds(p, 1)], ie.at[pl.ds(17 * sy, 1)], sems_c, p, 0,
                    {"tm": base + p, "sy": 1 - sy, "sx": 1 - sx})

    @pl.when(r == 15 * (1 - sy))
    def _():
        for p in everyone:
            to_row(p).start()
            to_corner(p).start()
    for p in everyone:
        to_column(p).start()
    for p in peers:
        send(so.at[p], inc.at[p], sems_o, p, p, {"tm": base + p}).wait()

    for c in range(cols):
        @pl.when(c > y)
        def _(c=c):
            send(ta, ca.at[y], sems_ca, c, y, {"tm": c * ROW + r}).wait_send()
            send(tb, cb.at[y], sems_cb, c, y, {"tm": c * ROW + r}).wait_send()

    before = inc[...].reshape(PIX, S)
    for f in range(T):
        state = loc[f] + fade[f] * before
        high = state.astype(BF16)
        low = (state - high.astype(F32)).astype(BF16)
        hid[f, pl.ds(1, H)] = jnp.concatenate([high, low], axis=1).reshape(H, W, C)

    for f in range(T):
        left = jnp.concatenate([hid[f, pl.ds(dy, H)].reshape(PIX, C) for dy in range(3)], axis=1)
        direct = skp[...] * xp[f, pl.ds(2, H)].reshape(PIX, C).astype(F32)
        acc[f] = shifted(dot(left, wc2[...]), 3, C, 1) + direct

    for c in edge_copies:
        c.wait()
    for p in everyone:
        send(se.at[pl.ds(p, 1)], ie.at[pl.ds(1 + p, 1)], sems_e, p, p, {"tm": base + p, "sx": 1 - sx}).wait()
    to_row(r).wait_recv()
    to_corner(r).wait_recv()

    @pl.when(r == 15 * (1 - sy))
    def _():
        for p in everyone:
            to_row(p).wait_send()
            to_corner(p).wait_send()
    state = ner[pl.ds(0, T)] + ner[pl.ds(T, T)] * ir[...].reshape(1, W, S)
    high = state.astype(BF16)
    hr2[...] = jnp.concatenate([high, (state - high.astype(F32)).astype(BF16)], axis=2)
    both = nec[...]
    state = both[:, :T] + both[:, T:] * ie[...]
    there = lax.broadcasted_iota(jnp.int32, (H + 2, 1, 1), 0) != 17 * sy
    state = jnp.where(there, state, 0.0)
    state = jnp.concatenate([state, jnp.zeros_like(state)], axis=1)
    high = state.astype(BF16)
    hc2[...] = jnp.concatenate([high, (state - high.astype(F32)).astype(BF16)], axis=2)
    first = pl.multiple_of(2 * C * (1 - sy), C)
    extra = shifted(dot(hr2[...].reshape(T * W, C), wc2[pl.ds(first, C), :]), 3, C, 1).reshape(T, W, C)
    at = pl.multiple_of(15 * W * (1 - sy), W)
    for f in range(T):
        acc[f, pl.ds(at, W), :] += extra[f]
    left = jnp.concatenate([hc2[pl.ds(dy, H)].reshape(8 * H, C) for dy in range(3)], axis=1)
    first = pl.multiple_of(2 * C * (1 - sx), C)
    side = dot(left, wc2[:, pl.ds(first, C)]).reshape(H, 8, C)
    at = pl.multiple_of(8 * (1 - sx), 8)
    outer = lax.broadcasted_iota(jnp.int32, (1, 8, C), 1) == 7 * (1 - sx)
    acc4 = acc.reshape(T, H, W, C)
    for f in range(T):
        acc4[f, :, pl.ds(at, 8), :] += jnp.where(outer, side[:, f:f + 1, :], 0.0)
    stores = []
    for f in range(T):
        done[f] = acc[f].reshape(H, W, C).astype(BF16)
        stores.append(pltpu.make_async_copy(done.at[f], out.at[f], store.at[f]))
        stores[f].start()
    for c in stores:
        c.wait()


def body(frames, in_kernel, dt_weight, rates, out_kernel, skip):
    cols = lax.axis_size("tm") // ROW
    hbm = pl.BlockSpec(memory_space=pltpu.HBM)

    def kernel(*refs):
        layer_kernel(cols, *refs)

    dma = pltpu.SemaphoreType.DMA
    chunk = (H, S)
    return pl.pallas_call(
        kernel,
        out_shape=jax.ShapeDtypeStruct(frames.shape, BF16),
        in_specs=[hbm] * 6,
        out_specs=hbm,
        scratch_shapes=[
            pltpu.VMEM((C,), BF16),
            pltpu.VMEM((1, S), F32),
            pltpu.VMEM((1, C), F32),
            pltpu.VMEM(chunk, F32),
            pltpu.VMEM((T, H + 4, W, C), BF16),
            pltpu.VMEM((5 * C, 5 * S), BF16),
            pltpu.VMEM((3 * C, 3 * C), BF16),
            pltpu.VMEM((T, 3, W, C), BF16),
            pltpu.VMEM((H + 4, 8, C), BF16),
            pltpu.VMEM((H, 8, C), BF16),
            pltpu.VMEM((T, PIX, S), F32),
            pltpu.VMEM((T, PIX, S), F32),
            pltpu.VMEM((T, PIX, S), F32),
            pltpu.VMEM((T, PIX, S), F32),
            pltpu.VMEM((T, H + 2, W, C), BF16),
            pltpu.VMEM((T, W, C), BF16),
            pltpu.VMEM((H + 2, 8, C), BF16),
            pltpu.VMEM((T, PIX, C), F32),
            pltpu.VMEM((T, H, W, C), BF16),
            pltpu.VMEM((2 * T, W, S), F32),
            pltpu.VMEM((H, 2 * T, S), F32),
            pltpu.VMEM((2 * T, W, S), F32),
            pltpu.VMEM((H + 2, 2 * T, S), F32),
            pltpu.VMEM((ROW, 1, S), F32),
            pltpu.VMEM((H + 2, 1, S), F32),
            pltpu.VMEM(chunk, F32),
            pltpu.VMEM((ROW,) + chunk, F32),
            pltpu.VMEM((ROW,) + chunk, F32),
            pltpu.VMEM((ROW,) + chunk, F32),
            pltpu.VMEM((ROW,) + chunk, F32),
            pltpu.VMEM((cols,) + chunk, F32),
            pltpu.VMEM((cols,) + chunk, F32),
            pltpu.VMEM(chunk, F32),
            pltpu.VMEM(chunk, F32),
            pltpu.VMEM((ROW,) + chunk, F32),
            pltpu.VMEM((ROW,) + chunk, F32),
            pltpu.SemaphoreType.REGULAR,
            pltpu.SemaphoreType.REGULAR,
            pltpu.SemaphoreType.REGULAR,
            dma((3,)),
            dma((T,)),
            dma,
            dma((25,)),
            dma((18,)),
            dma((2, 3)),
            dma((2, 3)),
            dma((2, ROW)),
            dma((2, ROW)),
            dma((2, cols)),
            dma((2, cols)),
            dma((2, ROW)),
            dma((2, ROW)),
            dma((2, ROW)),
            dma((2, ROW)),
        ],
        compiler_params=pltpu.CompilerParams(
            collective_id=0, has_side_effects=True, vmem_limit_bytes=67_000_000),
    )(frames, in_kernel.reshape(25, C, S), dt_weight, rates.reshape(1, S),
      out_kernel.reshape(9, S, C), skip.reshape(1, C))


def solution(mesh):
    return jax.shard_map(
        body,
        mesh=mesh,
        in_specs=(P("tm", "sy", "sx", None), P(), P(), P(), P(), P()),
        out_specs=P("tm", "sy", "sx", None),
        check_vma=False,
    )
```
